256 devices in a mesh: ctx: 32 (over z, x_lo, core), tp: 8 (over x_hi, y).
Axes of the slice: x: 4 (x_hi: 2, x_lo: 2; x = x_hi * 2 + x_lo), y: 4, z: 8, core: 2. Of those that a mesh axis runs over, the one named last changes fastest.
Arguments:
- record_lengths: int32 [16], replicated, may hold values from 1 to 3264, 6144 in all
- query_heads: bfloat16 [6144, 8192], P(('ctx', 'tp')), may hold values from -36 to 36
- key_heads: bfloat16 [6144, 1024], P(('ctx', 'tp')), may hold values from -36 to 36
- value_heads: bfloat16 [6144, 1024], P(('ctx', 'tp')), may hold values from -5 to 5
- out_grad: bfloat16 [6144, 8192], P(('ctx', 'tp')), may hold values from -5 to 5
- gate_input: bfloat16 [6144, 8192], P('ctx', 'tp'), may hold values from -5 to 5
- key_input: bfloat16 [6144, 8192], P('ctx', 'tp'), may hold values from -5 to 5
- value_input: bfloat16 [6144, 8192], P('ctx', 'tp'), may hold values from -5 to 5
- hyena_grad: bfloat16 [6144, 8192], P('ctx', 'tp'), may hold values from -5 to 5
- short_filter: float32 [3, 3, 8192], P(None, None, 'tp'), may hold values from -3 to 3
- long_filter: float32 [7, 512], P(None, 'tp'), may hold values from -3 to 3
Outputs:
- attn_out: bfloat16 [6144, 8192], P('ctx', 'tp')
- grad_query: bfloat16 [6144, 8192], P('ctx', 'tp')
- grad_key: bfloat16 [6144, 1024], P('ctx', 'tp')
- grad_value: bfloat16 [6144, 1024], P('ctx', 'tp')
- hyena_out: bfloat16 [6144, 8192], P('ctx', 'tp')
- grad_gate_in: bfloat16 [6144, 8192], P('ctx', 'tp')
- grad_key_in: bfloat16 [6144, 8192], P('ctx', 'tp')
- grad_value_in: bfloat16 [6144, 8192], P('ctx', 'tp')
The draws below stay inside these ranges and needn't reach their ends.
Inputs may be any that keep to these rules, and one draw needn't show every extreme that they name: `record_lengths`: the 16 records lie end to end and fill the 6144 tokens; the longest has exactly 3264 tokens.
All inputs are finite; a program needn't handle non-finite values.
Results may differ from the reference program's by a relative error of at most 0.035.
Values may be sent and summed in bfloat16 or wider, within the bound.
A program may use at most 64 MiB of HBM per device.

```python
import math
from functools import partial
import jax
import jax.numpy as jnp
import numpy as np
from jax import lax

HD = 128
QH = 64
KVH = 8
CH = 8192
GROUP = 16
TAPS = 7
SHORT = 3
TOK_DEV = 192
NREC = 16
LEN = 6144
MOST = 3264


def paired_heads(key):
    base = jax.random.fold_in(key, 11)
    parts = jax.random.split(base, 2)
    group = QH // KVH
    raw_keys = jax.random.truncated_normal(parts[0], -4.0, 4.0, (LEN, KVH, HD), jnp.float32)
    raw_queries = jax.random.truncated_normal(parts[1], -4.0, 4.0, (LEN, KVH, group, HD), jnp.float32)
    key_rows = raw_keys
    query_rows = raw_queries
    return (query_rows.reshape(LEN, QH * HD), key_rows.reshape(LEN, KVH * HD))


def draw_query_heads(key, part):
    return paired_heads(key)[0].astype(jnp.bfloat16)


def draw_key_heads(key, part):
    return paired_heads(key)[1].astype(jnp.bfloat16)


def shard_levels(own_key, extent, cuts, smallest, high):
    level = 1.0
    for position, shards_of in cuts:
        draws = jax.random.uniform(jax.random.fold_in(jax.random.fold_in(own_key, 6), position), (shards_of,), jnp.float32, smallest / len(cuts), high / len(cuts))
        level = level * jnp.repeat(jnp.exp(draws), extent[position] // shards_of).reshape((-1,) + (1,) * (len(extent) - 1 - position))
    return level


def split_up(number_of, total, reach, skew):
    weights = [(1 << 20) // math.isqrt(standing ** skew) + 1 for standing in range(2, number_of + 1)]
    rest, given = total - reach - (number_of - 1), [1] * (number_of - 1)
    while rest > 0:
        free = [i for i in range(number_of - 1) if given[i] < reach]
        whole, left = sum([weights[i] for i in free]), rest
        for i in free:
            extra = min(reach - given[i], max(1, left * weights[i] // whole), rest)
            given[i] = given[i] + extra
            rest = rest - extra
    return np.array([reach] + given)


def uneven_parts(rng, count, total, reach, lean):
    if count == 2:
        one = jax.random.randint(rng, (), max(1, total - reach), min(reach, total - 1) + 1)
        return jnp.stack([one, total - one])
    tallies = jnp.asarray(split_up(count, total, reach, lean), jnp.int32)
    pairs = (count - 1) // 2
    source_of, taker = tallies[1:1 + 2 * pairs:2], tallies[2:2 + 2 * pairs:2]
    margin = jnp.minimum(source_of - 1, reach - taker)
    moved = jax.random.randint(jax.random.fold_in(rng, 1), (pairs,), 0, 1 << 20) % (margin + 1)
    tallies = tallies.at[1:1 + 2 * pairs:2].set(source_of - moved).at[2:2 + 2 * pairs:2].set(taker + moved)
    return tallies[jax.random.permutation(jax.random.fold_in(rng, 2), count)]


def noise(own_key, dims, scale, bound, cuts=(), kind=jnp.bfloat16):
    gain = shard_levels(own_key, dims, cuts, -0.22, 0.18) if cuts else 1.0
    values = jax.random.normal(own_key, dims, jnp.float32) * scale * gain
    return jnp.minimum(jnp.maximum(values, -bound), bound).astype(kind)


def setup_inputs(seed: int = 0) -> dict:
    keys = jax.random.split(jax.random.key(seed), 12)
    record_lengths = uneven_parts(keys[0], NREC, LEN, MOST, 2).astype(jnp.int32)
    query_heads = draw_query_heads(jax.random.fold_in(keys[11], 71), 0)
    key_heads = draw_key_heads(jax.random.fold_in(keys[11], 71), 0)
    value_heads = noise(keys[3], (LEN, KVH * HD), 1.0, 5.0, ((0, 256),))
    out_grad = noise(keys[4], (LEN, QH * HD), 1.0, 5.0, ((0, 256),))
    gate_input = noise(keys[5], (LEN, CH), 1.0, 5.0, ((0, 32), (1, 8)))
    key_input = noise(keys[6], (LEN, CH), 1.0, 5.0, ((0, 32), (1, 8)))
    value_input = noise(keys[7], (LEN, CH), 1.0, 5.0, ((0, 32), (1, 8)))
    hyena_grad = noise(keys[8], (LEN, CH), 1.0, 5.0, ((0, 32), (1, 8)))
    short_filter = noise(keys[9], (3, SHORT, CH), 0.6, 3.0, ((2, 8),), jnp.float32)
    long_filter = noise(keys[10], (TAPS, CH // GROUP), 0.4, 3.0, ((1, 8),), jnp.float32)
    return dict(record_lengths=record_lengths, query_heads=query_heads, key_heads=key_heads, value_heads=value_heads, out_grad=out_grad, gate_input=gate_input, key_input=key_input, value_input=value_input, hyena_grad=hyena_grad, short_filter=short_filter, long_filter=long_filter)


def segment_ids(record_lengths, positions):
    ends = jnp.cumsum(record_lengths)
    starts = ends - record_lengths
    return lax.optimization_barrier(jnp.sum((starts[None, :] <= positions[:, None]).astype(jnp.int32), axis=1)) - 1

def bf16_round(values):
    return lax.optimization_barrier(values.astype(jnp.bfloat16)).astype(jnp.float32)

def attention(record_lengths, query_heads, key_heads, value_heads, out_grad):
    group = QH // KVH
    scale = HD ** (-0.5)
    blocks = LEN // TOK_DEV
    positions = jnp.arange(LEN, dtype=jnp.int32)
    segs = segment_ids(record_lengths, positions)
    q_all = query_heads.reshape(blocks, TOK_DEV, KVH, group, HD).transpose(2, 0, 1, 3, 4)
    g_all = out_grad.reshape(blocks, TOK_DEV, KVH, group, HD).transpose(2, 0, 1, 3, 4)
    k_all = key_heads.reshape(LEN, KVH, HD).transpose(1, 0, 2)
    v_all = value_heads.reshape(LEN, KVH, HD).transpose(1, 0, 2)
    q_pos = positions.reshape(blocks, TOK_DEV)
    q_seg = segs.reshape(blocks, TOK_DEV)

    def one_head(operands):
        q_head, g_head, k_head, v_head = operands
        key32 = k_head.astype(jnp.float32)
        val32 = v_head.astype(jnp.float32)

        def one_block(carry, block):
            dk_sum, dv_sum = carry
            q_blk, g_blk, pos_blk, seg_blk = block
            q32 = q_blk.astype(jnp.float32)
            g32 = g_blk.astype(jnp.float32)
            allowed = (positions[None, :] <= pos_blk[:, None]) & (segs[None, :] == seg_blk[:, None])
            allowed = allowed[None]
            scores = jnp.einsum('tgd,sd->gts', q32, key32) * scale
            peak = lax.optimization_barrier(jnp.max(jnp.where(allowed, scores, -jnp.inf), axis=2))
            weights = jnp.where(allowed, jnp.exp(scores - peak[:, :, None]), 0.0)
            total = lax.optimization_barrier(jnp.sum(weights, axis=2))
            mixed = jnp.einsum('gts,sd->gtd', bf16_round(weights), val32) / total[:, :, None]
            out_b = mixed.astype(jnp.bfloat16)
            lse = peak + jnp.log(total)
            delta = lax.optimization_barrier(jnp.sum(g32.transpose(1, 0, 2) * out_b.astype(jnp.float32), axis=2))
            probs = jnp.where(allowed, jnp.exp(scores - lse[:, :, None]), 0.0)
            probs_b = bf16_round(probs)
            dv_sum = dv_sum + jnp.einsum('gts,tgd->sd', probs_b, g32)
            dprobs = jnp.einsum('tgd,sd->gts', g32, val32)
            dscores = bf16_round(probs * (dprobs - delta[:, :, None]))
            dq_blk = scale * jnp.einsum('gts,sd->tgd', dscores, key32)
            dk_sum = dk_sum + scale * jnp.einsum('gts,tgd->sd', dscores, q32)
            return ((dk_sum, dv_sum), (out_b.transpose(1, 0, 2), dq_blk.astype(jnp.bfloat16)))
        zeros = jnp.zeros((LEN, HD), jnp.float32)
        sums, stacked = lax.scan(one_block, (zeros, zeros), (q_head, g_head, q_pos, q_seg))
        return (stacked[0], stacked[1], sums[0].astype(jnp.bfloat16), sums[1].astype(jnp.bfloat16))
    outs, dqs, dks, dvs = lax.map(one_head, (q_all, g_all, k_all, v_all))
    attn_out = outs.transpose(1, 2, 0, 3, 4).reshape(LEN, QH * HD)
    grad_query = dqs.transpose(1, 2, 0, 3, 4).reshape(LEN, QH * HD)
    grad_key = dks.transpose(1, 0, 2).reshape(LEN, KVH * HD)
    grad_value = dvs.transpose(1, 0, 2).reshape(LEN, KVH * HD)
    return (attn_out, grad_query, grad_key, grad_value)

def shifted(values, amount):
    return jnp.pad(values, ((amount, 0), (0, 0)))[:values.shape[0]]

def hyena_forward(short_filter, long_filter, gate_in, key_in, value_in):

    def featurize(values, taps):
        result = taps[0] * values
        for index in range(1, SHORT):
            result = result + taps[index] * shifted(values, index)
        return result
    gate_f = featurize(gate_in, short_filter[0])
    key_f = featurize(key_in, short_filter[1])
    value_f = featurize(value_in, short_filter[2])
    mixed = key_f * value_f
    per_channel = jnp.repeat(long_filter, GROUP, axis=1)
    conv = per_channel[0] * mixed
    for index in range(1, TAPS):
        conv = conv + per_channel[index] * shifted(mixed, index)
    return gate_f * conv

def reference(record_lengths, query_heads, key_heads, value_heads, out_grad, gate_input, key_input, value_input, hyena_grad, short_filter, long_filter):
    attn_out, grad_query, grad_key, grad_value = attention(record_lengths, query_heads, key_heads, value_heads, out_grad)
    forward = partial(hyena_forward, short_filter, long_filter)
    hyena_val, pullback = jax.vjp(forward, gate_input.astype(jnp.float32), key_input.astype(jnp.float32), value_input.astype(jnp.float32))
    grads = pullback(hyena_grad.astype(jnp.float32))
    return (attn_out, grad_query, grad_key, grad_value, hyena_val.astype(jnp.bfloat16), grads[0].astype(jnp.bfloat16), grads[1].astype(jnp.bfloat16), grads[2].astype(jnp.bfloat16))
```

```python
import jax
import jax.numpy as jnp
from jax import lax
from jax.sharding import PartitionSpec as P

HD = 128
QH = 64
KVH = 8
GROUP = 16
TAPS = 7
SHORT = 3
HALO = 8


NEG = -1e30


def padded_2(cells, sides, width):
    for axis, dim in sides:
        count = lax.axis_size(axis)
        ends = count - 1
        head = lax.slice_in_dim(cells, 0, width, axis=dim)
        tail = lax.slice_in_dim(cells, cells.shape[dim] - width, cells.shape[dim], axis=dim)
        cells = jnp.concatenate(
            [
                lax.ppermute(tail, axis, [(i, (i + 1) % count) for i in range(ends)]),
                cells,
                lax.ppermute(head, axis, [((i + 1) % count, i) for i in range(ends)]),
            ],
            axis=dim,
        )
    return cells


def hyena_local(padded, short_filter, long_filter, tokens):
    wide = padded.astype(jnp.float32)
    rows = wide.shape[0]
    lead = SHORT - 1
    per_channel = jnp.repeat(long_filter, GROUP, axis=1)

    def featurize(values, taps):
        result = taps[0] * values[lead:rows]
        for index in range(1, SHORT):
            result = result + taps[index] * values[lead - index : rows - index]
        return result

    gate_f = featurize(wide[:, 0], short_filter[0])
    key_f = featurize(wide[:, 1], short_filter[1])
    value_f = featurize(wide[:, 2], short_filter[2])
    mixed = key_f * value_f
    offset = HALO - lead
    span = rows - HALO
    conv = per_channel[0] * mixed[offset : offset + span]
    for index in range(1, TAPS):
        conv = conv + per_channel[index] * mixed[offset - index : offset - index + span]
    gate_c = gate_f[offset:]
    grad_c = wide[HALO:, 3]
    hyena_val = (gate_c[:tokens] * conv[:tokens]).astype(jnp.bfloat16)
    dconv = grad_c * gate_c
    dgate_f = grad_c * conv
    dmixed = per_channel[0] * dconv[0 : tokens + lead]
    for index in range(1, TAPS):
        dmixed = dmixed + per_channel[index] * dconv[index : index + tokens + lead]
    key_c = key_f[offset : offset + tokens + lead]
    value_c = value_f[offset : offset + tokens + lead]
    dkey_f = dmixed * value_c
    dvalue_f = dmixed * key_c

    def unfeaturize(grads, taps):
        result = taps[0] * grads[0:tokens]
        for index in range(1, SHORT):
            result = result + taps[index] * grads[index : index + tokens]
        return result.astype(jnp.bfloat16)

    return (
        hyena_val,
        unfeaturize(dgate_f, short_filter[0]),
        unfeaturize(dkey_f, short_filter[1]),
        unfeaturize(dvalue_f, short_filter[2]),
    )


def body(
    record_lengths,
    query_heads,
    key_heads,
    value_heads,
    out_grad,
    gate_input,
    key_input,
    value_input,
    hyena_grad,
    short_filter,
    long_filter,
):
    q_loc, k_loc, v_loc, g_loc = (
        lax.all_to_all(query_heads, "tp", split_axis=1, concat_axis=0, tiled=True),
        lax.all_to_all(key_heads, "tp", split_axis=1, concat_axis=0, tiled=True),
        lax.all_to_all(value_heads, "tp", split_axis=1, concat_axis=0, tiled=True),
        lax.all_to_all(out_grad, "tp", split_axis=1, concat_axis=0, tiled=True),
    )
    tokens = q_loc.shape[0]
    kv_width = k_loc.shape[1]
    kv_local = kv_width // HD
    group = QH // KVH
    scale = HD ** (-0.5)
    q_four = q_loc.reshape(tokens, kv_local, group, HD)
    g_four = g_loc.reshape(tokens, kv_local, group, HD)
    kv_pair = jnp.stack([k_loc, v_loc], axis=1)
    ends = jnp.cumsum(record_lengths)
    starts = ends - record_lengths

    def segment_of(positions):
        return jnp.sum((starts[None, :] <= positions[:, None]).astype(jnp.int32), axis=1) - 1

    own = lax.axis_index("ctx")
    q_start = own * tokens
    offsets = jnp.arange(tokens, dtype=jnp.int32)
    q_pos = q_start + offsets
    q_seg = segment_of(q_pos)
    first_seg = segment_of(jnp.reshape(q_start, (1,)))[0]

    def block_live(k_start):
        last_seg = segment_of(jnp.reshape(k_start + tokens - 1, (1,)))[0]
        return (
            (k_start >= 0) & (k_start <= q_start) & ((k_start == q_start) | (last_seg == first_seg))
        )

    def block_mask(k_start):
        k_pos = k_start + offsets
        k_seg = segment_of(k_pos)
        return ((k_pos[None, :] <= q_pos[:, None]) & (k_seg[None, :] == q_seg[:, None]))[None, None]

    def split_pair(block):
        return (
            block[:, 0].reshape(tokens, kv_local, HD),
            block[:, 1].reshape(tokens, kv_local, HD),
        )

    def block_scores(key_blk):
        return (
            jnp.einsum("tkgd,skd->kgts", q_four, key_blk, preferred_element_type=jnp.float32)
            * scale
        )

    def forward_add(state, block, k_start):
        peak, total, accum = state
        key_blk, val_blk = split_pair(block)
        allowed = block_mask(k_start)
        scores = block_scores(key_blk)
        new_peak = jnp.maximum(peak, jnp.max(jnp.where(allowed, scores, NEG), axis=3))
        factor = jnp.exp(peak - new_peak)
        weights = jnp.where(allowed, jnp.exp(scores - new_peak[..., None]), 0.0)
        total = total * factor + jnp.sum(weights, axis=3)
        accum = accum * factor[..., None] + jnp.einsum(
            "kgts,skd->kgtd",
            weights.astype(jnp.bfloat16),
            val_blk,
            preferred_element_type=jnp.float32,
        )
        return (new_peak, total, accum)

    gathered = lax.all_gather(kv_pair, "ctx", axis=0, tiled=True)
    count = gathered.shape[0] // tokens

    def fetch(index):
        return (lax.dynamic_slice_in_dim(gathered, index * tokens, tokens, 0), index * tokens)

    start_state = (
        jnp.full((kv_local, group, tokens), NEG, jnp.float32),
        jnp.zeros((kv_local, group, tokens), jnp.float32),
        jnp.zeros((kv_local, group, tokens, HD), jnp.float32),
    )

    def visit(index, state):
        block, k_start = fetch(index)
        return lax.cond(
            block_live(k_start),
            lambda inner: forward_add(inner, block, k_start),
            lambda inner: inner,
            state,
        )

    peak, total, accum = lax.fori_loop(0, count, visit, start_state)
    attn = (accum / total[..., None]).astype(jnp.bfloat16)
    attn_out = attn.transpose(2, 0, 1, 3).reshape(tokens, kv_local * group * HD)
    lse = peak + jnp.log(total)
    delta = jnp.sum(
        g_four.astype(jnp.float32).transpose(1, 2, 0, 3) * attn.astype(jnp.float32), axis=3
    )

    def backward_add(dq_sum, block, k_start):
        key_blk, val_blk = split_pair(block)
        allowed = block_mask(k_start)
        scores = block_scores(key_blk)
        probs = jnp.where(allowed, jnp.exp(scores - lse[..., None]), 0.0)
        dv_term = jnp.einsum(
            "kgts,tkgd->skd", probs.astype(jnp.bfloat16), g_four, preferred_element_type=jnp.float32
        )
        dprobs = jnp.einsum("tkgd,skd->kgts", g_four, val_blk, preferred_element_type=jnp.float32)
        dscores = (probs * (dprobs - delta[..., None])).astype(jnp.bfloat16)
        dq_sum = dq_sum + scale * jnp.einsum(
            "kgts,skd->tkgd", dscores, key_blk, preferred_element_type=jnp.float32
        )
        dk_term = scale * jnp.einsum(
            "kgts,tkgd->skd", dscores, q_four, preferred_element_type=jnp.float32
        )
        term = jnp.stack(
            [dk_term.reshape(tokens, kv_width), dv_term.reshape(tokens, kv_width)], axis=1
        )
        return (dq_sum, term)

    def visit_back(index, state):
        dq_sum, terms = state
        block, k_start = fetch(index)

        def skipped(dq_in):
            return (dq_in, jnp.zeros((tokens, 2, kv_width), jnp.float32))

        dq_sum, term = lax.cond(
            block_live(k_start), lambda dq_in: backward_add(dq_in, block, k_start), skipped, dq_sum
        )
        return (dq_sum, lax.dynamic_update_index_in_dim(terms, term, index, 0))

    start_back = (
        jnp.zeros((tokens, kv_local, group, HD), jnp.float32),
        jnp.zeros((count, tokens, 2, kv_width), jnp.float32),
    )
    dq_sum, terms = lax.fori_loop(0, count, visit_back, start_back)
    key_grads = jnp.sum(
        lax.all_to_all(
            terms.astype(jnp.bfloat16), "ctx", split_axis=0, concat_axis=0, tiled=True
        ).astype(jnp.float32),
        axis=0,
    )
    grad_query = dq_sum.reshape(tokens, kv_local * group * HD).astype(jnp.bfloat16)
    grad_key = key_grads[:, 0].astype(jnp.bfloat16)
    grad_value = key_grads[:, 1].astype(jnp.bfloat16)
    streams = jnp.stack([gate_input, key_input, value_input, hyena_grad], axis=1)
    padded = padded_2(streams, (("ctx", 0),), HALO)
    hyena_val, grad_gate, grad_keyx, grad_valuex = hyena_local(
        padded, short_filter, long_filter, streams.shape[0]
    )
    return (
        attn_out,
        grad_query,
        grad_key,
        grad_value,
        hyena_val,
        grad_gate,
        grad_keyx,
        grad_valuex,
    )


def solution(mesh):
    placed = (
        P(),
        P(("ctx", "tp"), None),
        P(("ctx", "tp"), None),
        P(("ctx", "tp"), None),
        P(("ctx", "tp"), None),
        P("ctx", "tp"),
        P("ctx", "tp"),
        P("ctx", "tp"),
        P("ctx", "tp"),
        P(None, None, "tp"),
        P(None, "tp"),
    )
    return jax.shard_map(
        body,
        mesh=mesh,
        in_specs=placed,
        out_specs=(
            P("ctx", "tp"),
            P("ctx", "tp"),
            P("ctx", "tp"),
            P("ctx", "tp"),
            P("ctx", "tp"),
            P("ctx", "tp"),
            P("ctx", "tp"),
            P("ctx", "tp"),
        ),
        check_vma=False,
    )
```

```python
import jax
import jax.numpy as jnp
from jax import lax
from jax.experimental import pallas as pl
from jax.experimental.pallas import tpu as pltpu
from jax.sharding import PartitionSpec as P

HD = 128
QH = 64
KVH = 8
GROUP = 16
TAPS = 7
SHORT = 3
HALO = 8


NEG = -1e30


def padded_2(cells, sides, width):
    for axis, dim in sides:
        count = lax.axis_size(axis)
        ends = count - 1
        head = lax.slice_in_dim(cells, 0, width, axis=dim)
        tail = lax.slice_in_dim(cells, cells.shape[dim] - width, cells.shape[dim], axis=dim)
        cells = jnp.concatenate(
            [
                lax.ppermute(tail, axis, [(i, (i + 1) % count) for i in range(ends)]),
                cells,
                lax.ppermute(head, axis, [((i + 1) % count, i) for i in range(ends)]),
            ],
            axis=dim,
        )
    return cells


def hyena_local(padded, short_filter, long_filter, tokens):
    wide = padded.astype(jnp.float32)
    rows = wide.shape[0]
    lead = SHORT - 1
    per_channel = jnp.repeat(long_filter, GROUP, axis=1)

    def featurize(values, taps):
        result = taps[0] * values[lead:rows]
        for index in range(1, SHORT):
            result = result + taps[index] * values[lead - index : rows - index]
        return result

    gate_f = featurize(wide[:, 0], short_filter[0])
    key_f = featurize(wide[:, 1], short_filter[1])
    value_f = featurize(wide[:, 2], short_filter[2])
    mixed = key_f * value_f
    offset = HALO - lead
    span = rows - HALO
    conv = per_channel[0] * mixed[offset : offset + span]
    for index in range(1, TAPS):
        conv = conv + per_channel[index] * mixed[offset - index : offset - index + span]
    gate_c = gate_f[offset:]
    grad_c = wide[HALO:, 3]
    hyena_val = (gate_c[:tokens] * conv[:tokens]).astype(jnp.bfloat16)
    dconv = grad_c * gate_c
    dgate_f = grad_c * conv
    dmixed = per_channel[0] * dconv[0 : tokens + lead]
    for index in range(1, TAPS):
        dmixed = dmixed + per_channel[index] * dconv[index : index + tokens + lead]
    key_c = key_f[offset : offset + tokens + lead]
    value_c = value_f[offset : offset + tokens + lead]
    dkey_f = dmixed * value_c
    dvalue_f = dmixed * key_c

    def unfeaturize(grads, taps):
        result = taps[0] * grads[0:tokens]
        for index in range(1, SHORT):
            result = result + taps[index] * grads[index : index + tokens]
        return result.astype(jnp.bfloat16)

    return (
        hyena_val,
        unfeaturize(dgate_f, short_filter[0]),
        unfeaturize(dkey_f, short_filter[1]),
        unfeaturize(dvalue_f, short_filter[2]),
    )


def attention_kernel(
    bounds_ref, q_ref, g_ref, kv_ref, qpos_ref, qstart_ref,
    out_ref, dq_ref, terms_ref,
    m_ref, l_ref, acc_ref, lse_ref, dl_ref, dqa_ref,
):
    tokens = q_ref.shape[0]
    heads = q_ref.shape[1] // HD
    scale = HD ** (-0.5)
    lo = bounds_ref[0]
    hi = bounds_ref[1]
    qpos = qpos_ref[...]
    qstart = qstart_ref[...]
    contract_last = (((1,), (1,)), ((), ()))
    contract_first = (((0,), (0,)), ((), ()))

    def allowed_of(j):
        kpos = j * tokens + lax.broadcasted_iota(jnp.int32, (1, tokens), 1)
        return (kpos <= qpos) & (kpos >= qstart)

    def key_value(j):
        rows = pl.ds(pl.multiple_of(j * tokens, 64), tokens)
        return kv_ref[rows, 0:HD], kv_ref[rows, HD : 2 * HD]

    m_ref[...] = jnp.full(m_ref.shape, NEG, jnp.float32)
    l_ref[...] = jnp.zeros(l_ref.shape, jnp.float32)
    acc_ref[...] = jnp.zeros(acc_ref.shape, jnp.float32)

    def forward_block(j, carry):
        key_blk, val_blk = key_value(j)
        allowed = allowed_of(j)
        for h in range(heads):
            cols = slice(h * HD, (h + 1) * HD)
            scores = (
                lax.dot_general(q_ref[:, cols], key_blk, contract_last, preferred_element_type=jnp.float32)
                * scale
            )
            m_old = m_ref[h]
            m_new = jnp.maximum(m_old, jnp.max(jnp.where(allowed, scores, NEG), axis=1, keepdims=True))
            weights = jnp.where(allowed, jnp.exp(scores - m_new), 0.0)
            factor = jnp.exp(m_old - m_new)
            l_ref[h] = l_ref[h] * factor + jnp.sum(weights, axis=1, keepdims=True)
            acc_ref[:, cols] = acc_ref[:, cols] * factor + jnp.dot(
                weights.astype(jnp.bfloat16), val_blk, preferred_element_type=jnp.float32
            )
            m_ref[h] = m_new
        return carry

    lax.fori_loop(lo, hi + 1, forward_block, 0)

    for h in range(heads):
        cols = slice(h * HD, (h + 1) * HD)
        attn = (acc_ref[:, cols] / l_ref[h]).astype(jnp.bfloat16)
        out_ref[:, cols] = attn
        lse_ref[h] = m_ref[h] + jnp.log(l_ref[h])
        dl_ref[h] = jnp.sum(
            g_ref[:, cols].astype(jnp.float32) * attn.astype(jnp.float32), axis=1, keepdims=True
        )
    dqa_ref[...] = jnp.zeros(dqa_ref.shape, jnp.float32)
    terms_ref[...] = jnp.zeros(terms_ref.shape, terms_ref.dtype)

    def backward_block(j, carry):
        key_blk, val_blk = key_value(j)
        allowed = allowed_of(j)
        dk = jnp.zeros((tokens, HD), jnp.float32)
        dv = jnp.zeros((tokens, HD), jnp.float32)
        for h in range(heads):
            cols = slice(h * HD, (h + 1) * HD)
            q_h = q_ref[:, cols]
            g_h = g_ref[:, cols]
            scores = (
                lax.dot_general(q_h, key_blk, contract_last, preferred_element_type=jnp.float32) * scale
            )
            probs = jnp.where(allowed, jnp.exp(scores - lse_ref[h]), 0.0)
            dv = dv + lax.dot_general(
                probs.astype(jnp.bfloat16), g_h, contract_first, preferred_element_type=jnp.float32
            )
            dprobs = lax.dot_general(g_h, val_blk, contract_last, preferred_element_type=jnp.float32)
            dscores = (probs * (dprobs - dl_ref[h])).astype(jnp.bfloat16)
            dqa_ref[:, cols] = dqa_ref[:, cols] + jnp.dot(
                dscores, key_blk, preferred_element_type=jnp.float32
            )
            dk = dk + lax.dot_general(dscores, q_h, contract_first, preferred_element_type=jnp.float32)
        terms_ref[j, :, 0:HD] = (dk * scale).astype(terms_ref.dtype)
        terms_ref[j, :, HD : 2 * HD] = dv.astype(terms_ref.dtype)
        return carry

    lax.fori_loop(lo, hi + 1, backward_block, 0)
    dq_ref[...] = (dqa_ref[...] * scale).astype(dq_ref.dtype)


def attention_local(bounds, q_loc, g_loc, kv_all, qpos, qstart):
    tokens, width = q_loc.shape
    heads = width // HD
    blocks = kv_all.shape[0] // tokens
    vmem = pl.BlockSpec(memory_space=pltpu.VMEM)
    return pl.pallas_call(
        attention_kernel,
        out_shape=(
            jax.ShapeDtypeStruct((tokens, width), jnp.bfloat16),
            jax.ShapeDtypeStruct((tokens, width), jnp.bfloat16),
            jax.ShapeDtypeStruct((blocks, tokens, 2 * HD), jnp.bfloat16),
        ),
        in_specs=[pl.BlockSpec(memory_space=pltpu.SMEM)] + [vmem] * 5,
        out_specs=(vmem, vmem, vmem),
        scratch_shapes=[
            pltpu.VMEM((heads, tokens, 1), jnp.float32),
            pltpu.VMEM((heads, tokens, 1), jnp.float32),
            pltpu.VMEM((tokens, width), jnp.float32),
            pltpu.VMEM((heads, tokens, 1), jnp.float32),
            pltpu.VMEM((heads, tokens, 1), jnp.float32),
            pltpu.VMEM((tokens, width), jnp.float32),
        ],
    )(bounds, q_loc, g_loc, kv_all, qpos, qstart)


def body(
    record_lengths,
    query_heads,
    key_heads,
    value_heads,
    out_grad,
    gate_input,
    key_input,
    value_input,
    hyena_grad,
    short_filter,
    long_filter,
):
    q_loc, k_loc, v_loc, g_loc = (
        lax.all_to_all(query_heads, "tp", split_axis=1, concat_axis=0, tiled=True),
        lax.all_to_all(key_heads, "tp", split_axis=1, concat_axis=0, tiled=True),
        lax.all_to_all(value_heads, "tp", split_axis=1, concat_axis=0, tiled=True),
        lax.all_to_all(out_grad, "tp", split_axis=1, concat_axis=0, tiled=True),
    )
    tokens = q_loc.shape[0]
    ends = jnp.cumsum(record_lengths)
    starts = ends - record_lengths

    def start_of(positions):
        seg = jnp.sum((starts[None, :] <= positions[:, None]).astype(jnp.int32), axis=1) - 1
        return jnp.take(starts, seg)

    own = lax.axis_index("ctx")
    q_start = own * tokens
    q_pos = q_start + jnp.arange(tokens, dtype=jnp.int32)
    q_rec = start_of(q_pos)
    bounds = jnp.stack([q_rec[0] // tokens, own]).astype(jnp.int32)
    kv_all = lax.all_gather(jnp.concatenate([k_loc, v_loc], axis=1), "ctx", axis=0, tiled=True)
    attn_out, grad_query, terms = attention_local(
        bounds, q_loc, g_loc, kv_all, q_pos[:, None], q_rec[:, None]
    )
    key_grads = jnp.sum(
        lax.all_to_all(terms, "ctx", split_axis=0, concat_axis=0, tiled=True).astype(jnp.float32),
        axis=0,
    )
    grad_key = key_grads[:, :HD].astype(jnp.bfloat16)
    grad_value = key_grads[:, HD:].astype(jnp.bfloat16)
    streams = jnp.stack([gate_input, key_input, value_input, hyena_grad], axis=1)
    padded = padded_2(streams, (("ctx", 0),), HALO)
    hyena_val, grad_gate, grad_keyx, grad_valuex = hyena_local(
        padded, short_filter, long_filter, streams.shape[0]
    )
    return (
        attn_out,
        grad_query,
        grad_key,
        grad_value,
        hyena_val,
        grad_gate,
        grad_keyx,
        grad_valuex,
    )


def solution(mesh):
    placed = (
        P(),
        P(("ctx", "tp"), None),
        P(("ctx", "tp"), None),
        P(("ctx", "tp"), None),
        P(("ctx", "tp"), None),
        P("ctx", "tp"),
        P("ctx", "tp"),
        P("ctx", "tp"),
        P("ctx", "tp"),
        P(None, None, "tp"),
        P(None, "tp"),
    )
    return jax.shard_map(
        body,
        mesh=mesh,
        in_specs=placed,
        out_specs=(
            P("ctx", "tp"),
            P("ctx", "tp"),
            P("ctx", "tp"),
            P("ctx", "tp"),
            P("ctx", "tp"),
            P("ctx", "tp"),
            P("ctx", "tp"),
            P("ctx", "tp"),
        ),
        check_vma=False,
    )
```

```python
import jax
import jax.numpy as jnp
from jax import lax
from jax.experimental import pallas as pl
from jax.experimental.pallas import tpu as pltpu
from jax.sharding import PartitionSpec as P

HD = 128
QH = 64
KVH = 8
GROUP = 16
TAPS = 7
SHORT = 3
HALO = 8
MOST = 3264


NEG = -1e30


def padded_2(cells, sides, width):
    for axis, dim in sides:
        count = lax.axis_size(axis)
        ends = count - 1
        head = lax.slice_in_dim(cells, 0, width, axis=dim)
        tail = lax.slice_in_dim(cells, cells.shape[dim] - width, cells.shape[dim], axis=dim)
        cells = jnp.concatenate(
            [
                lax.ppermute(tail, axis, [(i, (i + 1) % count) for i in range(ends)]),
                cells,
                lax.ppermute(head, axis, [((i + 1) % count, i) for i in range(ends)]),
            ],
            axis=dim,
        )
    return cells


def hyena_local(padded, short_filter, long_filter, tokens):
    wide = padded.astype(jnp.float32)
    rows = wide.shape[0]
    lead = SHORT - 1
    per_channel = jnp.repeat(long_filter, GROUP, axis=1)

    def featurize(values, taps):
        result = taps[0] * values[lead:rows]
        for index in range(1, SHORT):
            result = result + taps[index] * values[lead - index : rows - index]
        return result

    gate_f = featurize(wide[:, 0], short_filter[0])
    key_f = featurize(wide[:, 1], short_filter[1])
    value_f = featurize(wide[:, 2], short_filter[2])
    mixed = key_f * value_f
    offset = HALO - lead
    span = rows - HALO
    conv = per_channel[0] * mixed[offset : offset + span]
    for index in range(1, TAPS):
        conv = conv + per_channel[index] * mixed[offset - index : offset - index + span]
    gate_c = gate_f[offset:]
    grad_c = wide[HALO:, 3]
    hyena_val = (gate_c[:tokens] * conv[:tokens]).astype(jnp.bfloat16)
    dconv = grad_c * gate_c
    dgate_f = grad_c * conv
    dmixed = per_channel[0] * dconv[0 : tokens + lead]
    for index in range(1, TAPS):
        dmixed = dmixed + per_channel[index] * dconv[index : index + tokens + lead]
    key_c = key_f[offset : offset + tokens + lead]
    value_c = value_f[offset : offset + tokens + lead]
    dkey_f = dmixed * value_c
    dvalue_f = dmixed * key_c

    def unfeaturize(grads, taps):
        result = taps[0] * grads[0:tokens]
        for index in range(1, SHORT):
            result = result + taps[index] * grads[index : index + tokens]
        return result.astype(jnp.bfloat16)

    return (
        hyena_val,
        unfeaturize(dgate_f, short_filter[0]),
        unfeaturize(dkey_f, short_filter[1]),
        unfeaturize(dvalue_f, short_filter[2]),
    )


def attention_kernel(
    bounds_ref, q_ref, g_ref, kv_ref, qpos_ref, qstart_ref,
    out_ref, dq_ref, terms_ref,
    m_ref, l_ref, acc_ref, lse_ref, dl_ref, dqa_ref,
):
    tokens = q_ref.shape[0]
    heads = q_ref.shape[1] // HD
    scale = HD ** (-0.5)
    lo = bounds_ref[0]
    hi = bounds_ref[1]
    qpos = qpos_ref[...]
    qstart = qstart_ref[...]
    contract_last = (((1,), (1,)), ((), ()))
    contract_first = (((0,), (0,)), ((), ()))

    def allowed_of(j):
        kpos = j * tokens + lax.broadcasted_iota(jnp.int32, (1, tokens), 1)
        return (kpos <= qpos) & (kpos >= qstart)

    def key_value(j):
        rows = pl.ds(pl.multiple_of(j * tokens, 64), tokens)
        return kv_ref[rows, 0:HD], kv_ref[rows, HD : 2 * HD]

    m_ref[...] = jnp.full(m_ref.shape, NEG, jnp.float32)
    l_ref[...] = jnp.zeros(l_ref.shape, jnp.float32)
    acc_ref[...] = jnp.zeros(acc_ref.shape, jnp.float32)

    def forward_block(j, carry):
        key_blk, val_blk = key_value(j)
        allowed = allowed_of(j)
        for h in range(heads):
            cols = slice(h * HD, (h + 1) * HD)
            scores = (
                lax.dot_general(q_ref[:, cols], key_blk, contract_last, preferred_element_type=jnp.float32)
                * scale
            )
            m_old = m_ref[h]
            m_new = jnp.maximum(m_old, jnp.max(jnp.where(allowed, scores, NEG), axis=1, keepdims=True))
            weights = jnp.where(allowed, jnp.exp(scores - m_new), 0.0)
            factor = jnp.exp(m_old - m_new)
            l_ref[h] = l_ref[h] * factor + jnp.sum(weights, axis=1, keepdims=True)
            acc_ref[:, cols] = acc_ref[:, cols] * factor + jnp.dot(
                weights.astype(jnp.bfloat16), val_blk, preferred_element_type=jnp.float32
            )
            m_ref[h] = m_new
        return carry

    lax.fori_loop(lo, hi + 1, forward_block, 0)

    for h in range(heads):
        cols = slice(h * HD, (h + 1) * HD)
        attn = (acc_ref[:, cols] / l_ref[h]).astype(jnp.bfloat16)
        out_ref[:, cols] = attn
        lse_ref[h] = m_ref[h] + jnp.log(l_ref[h])
        dl_ref[h] = jnp.sum(
            g_ref[:, cols].astype(jnp.float32) * attn.astype(jnp.float32), axis=1, keepdims=True
        )
    dqa_ref[...] = jnp.zeros(dqa_ref.shape, jnp.float32)
    terms_ref[...] = jnp.zeros(terms_ref.shape, terms_ref.dtype)

    def backward_block(j, carry):
        key_blk, val_blk = key_value(j)
        allowed = allowed_of(j)
        dk = jnp.zeros((tokens, HD), jnp.float32)
        dv = jnp.zeros((tokens, HD), jnp.float32)
        for h in range(heads):
            cols = slice(h * HD, (h + 1) * HD)
            q_h = q_ref[:, cols]
            g_h = g_ref[:, cols]
            scores = (
                lax.dot_general(q_h, key_blk, contract_last, preferred_element_type=jnp.float32) * scale
            )
            probs = jnp.where(allowed, jnp.exp(scores - lse_ref[h]), 0.0)
            dv = dv + lax.dot_general(
                probs.astype(jnp.bfloat16), g_h, contract_first, preferred_element_type=jnp.float32
            )
            dprobs = lax.dot_general(g_h, val_blk, contract_last, preferred_element_type=jnp.float32)
            dscores = (probs * (dprobs - dl_ref[h])).astype(jnp.bfloat16)
            dqa_ref[:, cols] = dqa_ref[:, cols] + jnp.dot(
                dscores, key_blk, preferred_element_type=jnp.float32
            )
            dk = dk + lax.dot_general(dscores, q_h, contract_first, preferred_element_type=jnp.float32)
        terms_ref[hi - j, :, 0:HD] = (dk * scale).astype(terms_ref.dtype)
        terms_ref[hi - j, :, HD : 2 * HD] = dv.astype(terms_ref.dtype)
        return carry

    lax.fori_loop(lo, hi + 1, backward_block, 0)
    dq_ref[...] = (dqa_ref[...] * scale).astype(dq_ref.dtype)


def attention_local(bounds, q_loc, g_loc, kv_all, qpos, qstart, window):
    tokens, width = q_loc.shape
    heads = width // HD
    vmem = pl.BlockSpec(memory_space=pltpu.VMEM)
    return pl.pallas_call(
        attention_kernel,
        out_shape=(
            jax.ShapeDtypeStruct((tokens, width), jnp.bfloat16),
            jax.ShapeDtypeStruct((tokens, width), jnp.bfloat16),
            jax.ShapeDtypeStruct((window, tokens, 2 * HD), jnp.float32),
        ),
        in_specs=[pl.BlockSpec(memory_space=pltpu.SMEM)] + [vmem] * 5,
        out_specs=(vmem, vmem, vmem),
        scratch_shapes=[
            pltpu.VMEM((heads, tokens, 1), jnp.float32),
            pltpu.VMEM((heads, tokens, 1), jnp.float32),
            pltpu.VMEM((tokens, width), jnp.float32),
            pltpu.VMEM((heads, tokens, 1), jnp.float32),
            pltpu.VMEM((heads, tokens, 1), jnp.float32),
            pltpu.VMEM((tokens, width), jnp.float32),
        ],
    )(bounds, q_loc, g_loc, kv_all, qpos, qstart)


def window_reduce(terms, axis):
    width = terms.shape[0]
    count = lax.axis_size(axis)
    levels = max(1, (width - 1).bit_length())
    need = [None] * (levels + 1)
    need[levels] = [0]
    for k in reversed(range(levels)):
        step = 1 << k
        need[k] = sorted(set(need[k + 1]) | {e + step for e in need[k + 1] if e + step < width})
    held = {e: terms[e] for e in range(width)}
    for k in range(levels):
        step = 1 << k
        pairs = [e for e in need[k + 1] if e + step < width]
        if pairs and step < count:
            sent = jnp.stack([held[e + step] for e in pairs]).astype(jnp.bfloat16)
            got = lax.ppermute(sent, axis, [(i, i - step) for i in range(step, count)])
            for i, e in enumerate(pairs):
                held[e] = held[e] + got[i].astype(jnp.float32)
        held = {e: held[e] for e in need[k + 1]}
    return held[0]


def body(
    record_lengths,
    query_heads,
    key_heads,
    value_heads,
    out_grad,
    gate_input,
    key_input,
    value_input,
    hyena_grad,
    short_filter,
    long_filter,
):
    tp = lax.axis_size("tp")
    rows = query_heads.shape[0]
    pieces = [query_heads, key_heads, value_heads, out_grad]
    widths = [x.shape[1] // tp for x in pieces]
    joined = jnp.concatenate([x.reshape(rows, tp, w) for x, w in zip(pieces, widths)], axis=2)
    joined = lax.all_to_all(joined, "tp", split_axis=1, concat_axis=0, tiled=True)
    joined = joined.reshape(rows * tp, sum(widths))
    cuts = [0]
    for w in widths:
        cuts.append(cuts[-1] + w)
    q_loc, k_loc, v_loc, g_loc = [joined[:, a:b] for a, b in zip(cuts[:-1], cuts[1:])]
    tokens = q_loc.shape[0]
    ends = jnp.cumsum(record_lengths)
    starts = ends - record_lengths

    def start_of(positions):
        seg = jnp.sum((starts[None, :] <= positions[:, None]).astype(jnp.int32), axis=1) - 1
        return jnp.take(starts, seg)

    own = lax.axis_index("ctx")
    q_start = own * tokens
    q_pos = q_start + jnp.arange(tokens, dtype=jnp.int32)
    q_rec = start_of(q_pos)
    window = (MOST - 1) // tokens + 2
    first = jnp.maximum(q_rec[0] // tokens, own - (window - 1))
    bounds = jnp.stack([first, own]).astype(jnp.int32)
    kv_all = lax.all_gather(jnp.concatenate([k_loc, v_loc], axis=1), "ctx", axis=0, tiled=True)
    attn_out, grad_query, terms = attention_local(
        bounds, q_loc, g_loc, kv_all, q_pos[:, None], q_rec[:, None], window
    )
    key_grads = window_reduce(terms, "ctx")
    grad_key = key_grads[:, :HD].astype(jnp.bfloat16)
    grad_value = key_grads[:, HD:].astype(jnp.bfloat16)
    streams = jnp.stack([gate_input, key_input, value_input, hyena_grad], axis=1)
    padded = padded_2(streams, (("ctx", 0),), HALO)
    hyena_val, grad_gate, grad_keyx, grad_valuex = hyena_local(
        padded, short_filter, long_filter, streams.shape[0]
    )
    return (
        attn_out,
        grad_query,
        grad_key,
        grad_value,
        hyena_val,
        grad_gate,
        grad_keyx,
        grad_valuex,
    )


def solution(mesh):
    placed = (
        P(),
        P(("ctx", "tp"), None),
        P(("ctx", "tp"), None),
        P(("ctx", "tp"), None),
        P(("ctx", "tp"), None),
        P("ctx", "tp"),
        P("ctx", "tp"),
        P("ctx", "tp"),
        P("ctx", "tp"),
        P(None, None, "tp"),
        P(None, "tp"),
    )
    return jax.shard_map(
        body,
        mesh=mesh,
        in_specs=placed,
        out_specs=(
            P("ctx", "tp"),
            P("ctx", "tp"),
            P("ctx", "tp"),
            P("ctx", "tp"),
            P("ctx", "tp"),
            P("ctx", "tp"),
            P("ctx", "tp"),
            P("ctx", "tp"),
        ),
        check_vma=False,
    )
```

```python
import functools

import jax
import jax.numpy as jnp
from jax import lax
from jax.experimental import pallas as pl
from jax.experimental.pallas import tpu as pltpu
from jax.sharding import PartitionSpec as P

HD = 128
QH = 64
KVH = 8
GROUP = 16
TAPS = 7
SHORT = 3
HALO = 8
MOST = 3264


NEG = -1e30


def padded_2(cells, sides, width):
    for axis, dim in sides:
        count = lax.axis_size(axis)
        ends = count - 1
        head = lax.slice_in_dim(cells, 0, width, axis=dim)
        tail = lax.slice_in_dim(cells, cells.shape[dim] - width, cells.shape[dim], axis=dim)
        cells = jnp.concatenate(
            [
                lax.ppermute(tail, axis, [(i, (i + 1) % count) for i in range(ends)]),
                cells,
                lax.ppermute(head, axis, [((i + 1) % count, i) for i in range(ends)]),
            ],
            axis=dim,
        )
    return cells


def hyena_local(padded, short_filter, long_filter, tokens):
    wide = padded.astype(jnp.float32)
    rows = wide.shape[0]
    lead = SHORT - 1
    per_channel = jnp.repeat(long_filter, GROUP, axis=1)

    def featurize(values, taps):
        result = taps[0] * values[lead:rows]
        for index in range(1, SHORT):
            result = result + taps[index] * values[lead - index : rows - index]
        return result

    gate_f = featurize(wide[:, 0], short_filter[0])
    key_f = featurize(wide[:, 1], short_filter[1])
    value_f = featurize(wide[:, 2], short_filter[2])
    mixed = key_f * value_f
    offset = HALO - lead
    span = rows - HALO
    conv = per_channel[0] * mixed[offset : offset + span]
    for index in range(1, TAPS):
        conv = conv + per_channel[index] * mixed[offset - index : offset - index + span]
    gate_c = gate_f[offset:]
    grad_c = wide[HALO:, 3]
    hyena_val = (gate_c[:tokens] * conv[:tokens]).astype(jnp.bfloat16)
    dconv = grad_c * gate_c
    dgate_f = grad_c * conv
    dmixed = per_channel[0] * dconv[0 : tokens + lead]
    for index in range(1, TAPS):
        dmixed = dmixed + per_channel[index] * dconv[index : index + tokens + lead]
    key_c = key_f[offset : offset + tokens + lead]
    value_c = value_f[offset : offset + tokens + lead]
    dkey_f = dmixed * value_c
    dvalue_f = dmixed * key_c

    def unfeaturize(grads, taps):
        result = taps[0] * grads[0:tokens]
        for index in range(1, SHORT):
            result = result + taps[index] * grads[index : index + tokens]
        return result.astype(jnp.bfloat16)

    return (
        hyena_val,
        unfeaturize(dgate_f, short_filter[0]),
        unfeaturize(dkey_f, short_filter[1]),
        unfeaturize(dvalue_f, short_filter[2]),
    )


def attention_kernel(
    bounds_ref, q_ref, g_ref, kv_ref, qpos_ref, qstart_ref,
    out_ref, dq_ref, terms_ref,
    m_ref, l_ref, acc_ref, lse_ref, dl_ref, dqa_ref,
):
    tokens = q_ref.shape[0]
    heads = q_ref.shape[1] // HD
    scale = HD ** (-0.5)
    lo = bounds_ref[0]
    hi = bounds_ref[1]
    qpos = qpos_ref[...]
    qstart = qstart_ref[...]
    contract_last = (((1,), (1,)), ((), ()))
    contract_first = (((0,), (0,)), ((), ()))

    def allowed_of(j):
        kpos = j * tokens + lax.broadcasted_iota(jnp.int32, (1, tokens), 1)
        return (kpos <= qpos) & (kpos >= qstart)

    def key_value(j):
        rows = pl.ds(pl.multiple_of(j * tokens, 64), tokens)
        return kv_ref[rows, 0:HD], kv_ref[rows, HD : 2 * HD]

    m_ref[...] = jnp.full(m_ref.shape, NEG, jnp.float32)
    l_ref[...] = jnp.zeros(l_ref.shape, jnp.float32)
    acc_ref[...] = jnp.zeros(acc_ref.shape, jnp.float32)

    def forward_block(j, carry):
        key_blk, val_blk = key_value(j)
        allowed = allowed_of(j)
        for h in range(heads):
            cols = slice(h * HD, (h + 1) * HD)
            scores = (
                lax.dot_general(q_ref[:, cols], key_blk, contract_last, preferred_element_type=jnp.float32)
                * scale
            )
            m_old = m_ref[h]
            m_new = jnp.maximum(m_old, jnp.max(jnp.where(allowed, scores, NEG), axis=1, keepdims=True))
            weights = jnp.where(allowed, jnp.exp(scores - m_new), 0.0)
            factor = jnp.exp(m_old - m_new)
            l_ref[h] = l_ref[h] * factor + jnp.sum(weights, axis=1, keepdims=True)
            acc_ref[:, cols] = acc_ref[:, cols] * factor + jnp.dot(
                weights.astype(jnp.bfloat16), val_blk, preferred_element_type=jnp.float32
            )
            m_ref[h] = m_new
        return carry

    lax.fori_loop(lo, hi + 1, forward_block, 0)

    for h in range(heads):
        cols = slice(h * HD, (h + 1) * HD)
        attn = (acc_ref[:, cols] / l_ref[h]).astype(jnp.bfloat16)
        out_ref[:, cols] = attn
        lse_ref[h] = m_ref[h] + jnp.log(l_ref[h])
        dl_ref[h] = jnp.sum(
            g_ref[:, cols].astype(jnp.float32) * attn.astype(jnp.float32), axis=1, keepdims=True
        )
    dqa_ref[...] = jnp.zeros(dqa_ref.shape, jnp.float32)
    terms_ref[...] = jnp.zeros(terms_ref.shape, terms_ref.dtype)

    def backward_block(j, carry):
        key_blk, val_blk = key_value(j)
        allowed = allowed_of(j)
        dk = jnp.zeros((tokens, HD), jnp.float32)
        dv = jnp.zeros((tokens, HD), jnp.float32)
        for h in range(heads):
            cols = slice(h * HD, (h + 1) * HD)
            q_h = q_ref[:, cols]
            g_h = g_ref[:, cols]
            scores = (
                lax.dot_general(q_h, key_blk, contract_last, preferred_element_type=jnp.float32) * scale
            )
            probs = jnp.where(allowed, jnp.exp(scores - lse_ref[h]), 0.0)
            dv = dv + lax.dot_general(
                probs.astype(jnp.bfloat16), g_h, contract_first, preferred_element_type=jnp.float32
            )
            dprobs = lax.dot_general(g_h, val_blk, contract_last, preferred_element_type=jnp.float32)
            dscores = (probs * (dprobs - dl_ref[h])).astype(jnp.bfloat16)
            dqa_ref[:, cols] = dqa_ref[:, cols] + jnp.dot(
                dscores, key_blk, preferred_element_type=jnp.float32
            )
            dk = dk + lax.dot_general(dscores, q_h, contract_first, preferred_element_type=jnp.float32)
        terms_ref[hi - j, :, 0:HD] = (dk * scale).astype(terms_ref.dtype)
        terms_ref[hi - j, :, HD : 2 * HD] = dv.astype(terms_ref.dtype)
        return carry

    lax.fori_loop(lo, hi + 1, backward_block, 0)
    dq_ref[...] = (dqa_ref[...] * scale).astype(dq_ref.dtype)


def attention_local(bounds, q_loc, g_loc, kv_all, qpos, qstart, window):
    tokens, width = q_loc.shape
    heads = width // HD
    vmem = pl.BlockSpec(memory_space=pltpu.VMEM)
    return pl.pallas_call(
        attention_kernel,
        out_shape=(
            jax.ShapeDtypeStruct((tokens, width), jnp.bfloat16),
            jax.ShapeDtypeStruct((tokens, width), jnp.bfloat16),
            jax.ShapeDtypeStruct((window, tokens, 2 * HD), jnp.float32),
        ),
        in_specs=[pl.BlockSpec(memory_space=pltpu.SMEM)] + [vmem] * 5,
        out_specs=(vmem, vmem, vmem),
        scratch_shapes=[
            pltpu.VMEM((heads, tokens, 1), jnp.float32),
            pltpu.VMEM((heads, tokens, 1), jnp.float32),
            pltpu.VMEM((tokens, width), jnp.float32),
            pltpu.VMEM((heads, tokens, 1), jnp.float32),
            pltpu.VMEM((heads, tokens, 1), jnp.float32),
            pltpu.VMEM((tokens, width), jnp.float32),
        ],
    )(bounds, q_loc, g_loc, kv_all, qpos, qstart)


def window_stages(width):
    levels = max(1, (width - 1).bit_length())
    need = [None] * (levels + 1)
    need[levels] = [0]
    for k in reversed(range(levels)):
        step = 1 << k
        need[k] = sorted(set(need[k + 1]) | {e + step for e in need[k + 1] if e + step < width})
    return [[e for e in need[k + 1] if e + step < width] for k, step in enumerate(1 << k for k in range(levels))]


def reduce_kernel(stages, count, terms_ref, out_ref, held, *rest):
    depth = len(stages)
    send_bufs, recv_bufs = rest[:depth], rest[depth : 2 * depth]
    send_sem, recv_sem = rest[2 * depth], rest[2 * depth + 1]
    me = lax.axis_index("ctx")
    held[...] = terms_ref[...]
    for k, pairs in enumerate(stages):
        step = 1 << k
        copy = pltpu.make_async_remote_copy(
            src_ref=send_bufs[k],
            dst_ref=recv_bufs[k],
            send_sem=send_sem.at[k],
            recv_sem=recv_sem.at[k],
            device_id={"ctx": (me - step + count) % count},
            device_id_type=pl.DeviceIdType.MESH,
        )

        @pl.when(me >= step)
        def _():
            for i, e in enumerate(pairs):
                send_bufs[k][i] = held[e + step].astype(jnp.bfloat16)
            copy.start()

        @pl.when(me + step < count)
        def _():
            copy.wait_recv()
            for i, e in enumerate(pairs):
                held[e] = held[e] + recv_bufs[k][i].astype(jnp.float32)

        @pl.when(me >= step)
        def _():
            copy.wait_send()

    out_ref[...] = held[0]


def window_reduce(terms, axis):
    width, tokens, cols = terms.shape
    count = lax.axis_size(axis)
    stages = [pairs for k, pairs in enumerate(window_stages(width)) if (1 << k) < count]
    vmem = pl.BlockSpec(memory_space=pltpu.VMEM)
    bufs = [pltpu.VMEM((len(p), tokens, cols), jnp.bfloat16) for p in stages]
    return pl.pallas_call(
        functools.partial(reduce_kernel, stages, count),
        out_shape=jax.ShapeDtypeStruct((tokens, cols), jnp.float32),
        in_specs=[vmem],
        out_specs=vmem,
        scratch_shapes=[pltpu.VMEM((width, tokens, cols), jnp.float32)]
        + bufs
        + bufs
        + [pltpu.SemaphoreType.DMA((len(stages),)), pltpu.SemaphoreType.DMA((len(stages),))],
        compiler_params=pltpu.CompilerParams(has_side_effects=True),
    )(terms)


def body(
    record_lengths,
    query_heads,
    key_heads,
    value_heads,
    out_grad,
    gate_input,
    key_input,
    value_input,
    hyena_grad,
    short_filter,
    long_filter,
):
    tp = lax.axis_size("tp")
    rows = query_heads.shape[0]
    pieces = [query_heads, key_heads, value_heads, out_grad]
    widths = [x.shape[1] // tp for x in pieces]
    joined = jnp.concatenate([x.reshape(rows, tp, w) for x, w in zip(pieces, widths)], axis=2)
    joined = lax.all_to_all(joined, "tp", split_axis=1, concat_axis=0, tiled=True)
    joined = joined.reshape(rows * tp, sum(widths))
    cuts = [0]
    for w in widths:
        cuts.append(cuts[-1] + w)
    q_loc, k_loc, v_loc, g_loc = [joined[:, a:b] for a, b in zip(cuts[:-1], cuts[1:])]
    tokens = q_loc.shape[0]
    ends = jnp.cumsum(record_lengths)
    starts = ends - record_lengths

    def start_of(positions):
        seg = jnp.sum((starts[None, :] <= positions[:, None]).astype(jnp.int32), axis=1) - 1
        return jnp.take(starts, seg)

    own = lax.axis_index("ctx")
    q_start = own * tokens
    q_pos = q_start + jnp.arange(tokens, dtype=jnp.int32)
    q_rec = start_of(q_pos)
    window = (MOST - 1) // tokens + 2
    first = jnp.maximum(q_rec[0] // tokens, own - (window - 1))
    bounds = jnp.stack([first, own]).astype(jnp.int32)
    kv_all = lax.all_gather(jnp.concatenate([k_loc, v_loc], axis=1), "ctx", axis=0, tiled=True)
    attn_out, grad_query, terms = attention_local(
        bounds, q_loc, g_loc, kv_all, q_pos[:, None], q_rec[:, None], window
    )
    key_grads = window_reduce(terms, "ctx")
    grad_key = key_grads[:, :HD].astype(jnp.bfloat16)
    grad_value = key_grads[:, HD:].astype(jnp.bfloat16)
    streams = jnp.stack([gate_input, key_input, value_input, hyena_grad], axis=1)
    padded = padded_2(streams, (("ctx", 0),), HALO)
    hyena_val, grad_gate, grad_keyx, grad_valuex = hyena_local(
        padded, short_filter, long_filter, streams.shape[0]
    )
    return (
        attn_out,
        grad_query,
        grad_key,
        grad_value,
        hyena_val,
        grad_gate,
        grad_keyx,
        grad_valuex,
    )


def solution(mesh):
    placed = (
        P(),
        P(("ctx", "tp"), None),
        P(("ctx", "tp"), None),
        P(("ctx", "tp"), None),
        P(("ctx", "tp"), None),
        P("ctx", "tp"),
        P("ctx", "tp"),
        P("ctx", "tp"),
        P("ctx", "tp"),
        P(None, None, "tp"),
        P(None, "tp"),
    )
    return jax.shard_map(
        body,
        mesh=mesh,
        in_specs=placed,
        out_specs=(
            P("ctx", "tp"),
            P("ctx", "tp"),
            P("ctx", "tp"),
            P("ctx", "tp"),
            P("ctx", "tp"),
            P("ctx", "tp"),
            P("ctx", "tp"),
            P("ctx", "tp"),
        ),
        check_vma=False,
    )
```

```python
import functools

import jax
import jax.numpy as jnp
from jax import lax
from jax.experimental import pallas as pl
from jax.experimental.pallas import tpu as pltpu
from jax.sharding import PartitionSpec as P

HD = 128
QH = 64
KVH = 8
GROUP = 16
TAPS = 7
SHORT = 3
HALO = 8
MOST = 3264


NEG = -1e30


def padded_2(cells, sides, width):
    for axis, dim in sides:
        count = lax.axis_size(axis)
        ends = count - 1
        head = lax.slice_in_dim(cells, 0, width, axis=dim)
        tail = lax.slice_in_dim(cells, cells.shape[dim] - width, cells.shape[dim], axis=dim)
        cells = jnp.concatenate(
            [
                lax.ppermute(tail, axis, [(i, (i + 1) % count) for i in range(ends)]),
                cells,
                lax.ppermute(head, axis, [((i + 1) % count, i) for i in range(ends)]),
            ],
            axis=dim,
        )
    return cells


def hyena_local(padded, short_filter, long_filter, tokens):
    wide = padded.astype(jnp.float32)
    rows = wide.shape[0]
    lead = SHORT - 1
    per_channel = jnp.repeat(long_filter, GROUP, axis=1)

    def featurize(values, taps):
        result = taps[0] * values[lead:rows]
        for index in range(1, SHORT):
            result = result + taps[index] * values[lead - index : rows - index]
        return result

    gate_f = featurize(wide[:, 0], short_filter[0])
    key_f = featurize(wide[:, 1], short_filter[1])
    value_f = featurize(wide[:, 2], short_filter[2])
    mixed = key_f * value_f
    offset = HALO - lead
    span = rows - HALO
    conv = per_channel[0] * mixed[offset : offset + span]
    for index in range(1, TAPS):
        conv = conv + per_channel[index] * mixed[offset - index : offset - index + span]
    gate_c = gate_f[offset:]
    grad_c = wide[HALO:, 3]
    hyena_val = (gate_c[:tokens] * conv[:tokens]).astype(jnp.bfloat16)
    dconv = grad_c * gate_c
    dgate_f = grad_c * conv
    dmixed = per_channel[0] * dconv[0 : tokens + lead]
    for index in range(1, TAPS):
        dmixed = dmixed + per_channel[index] * dconv[index : index + tokens + lead]
    key_c = key_f[offset : offset + tokens + lead]
    value_c = value_f[offset : offset + tokens + lead]
    dkey_f = dmixed * value_c
    dvalue_f = dmixed * key_c

    def unfeaturize(grads, taps):
        result = taps[0] * grads[0:tokens]
        for index in range(1, SHORT):
            result = result + taps[index] * grads[index : index + tokens]
        return result.astype(jnp.bfloat16)

    return (
        hyena_val,
        unfeaturize(dgate_f, short_filter[0]),
        unfeaturize(dkey_f, short_filter[1]),
        unfeaturize(dvalue_f, short_filter[2]),
    )


def attention_kernel(
    bounds_ref, q_ref, g_ref, kv_ref, qpos_ref, qstart_ref,
    out_ref, dq_ref, terms_ref,
    m_ref, l_ref, acc_ref, lse_ref, dl_ref, dqa_ref,
):
    tokens = q_ref.shape[0]
    heads = q_ref.shape[1] // HD
    scale = HD ** (-0.5)
    lo = bounds_ref[0]
    hi = bounds_ref[1]
    qpos = qpos_ref[...]
    qstart = qstart_ref[...]
    contract_last = (((1,), (1,)), ((), ()))
    contract_first = (((0,), (0,)), ((), ()))

    def allowed_of(j):
        kpos = j * tokens + lax.broadcasted_iota(jnp.int32, (1, tokens), 1)
        return (kpos <= qpos) & (kpos >= qstart)

    def key_value(j):
        rows = pl.ds(pl.multiple_of(j * tokens, 64), tokens)
        return kv_ref[rows, 0:HD], kv_ref[rows, HD : 2 * HD]

    m_ref[...] = jnp.full(m_ref.shape, NEG, jnp.float32)
    l_ref[...] = jnp.zeros(l_ref.shape, jnp.float32)
    acc_ref[...] = jnp.zeros(acc_ref.shape, jnp.float32)

    def forward_block(j, carry):
        key_blk, val_blk = key_value(j)
        allowed = allowed_of(j)
        for h in range(heads):
            cols = slice(h * HD, (h + 1) * HD)
            scores = (
                lax.dot_general(q_ref[:, cols], key_blk, contract_last, preferred_element_type=jnp.float32)
                * scale
            )
            m_old = m_ref[h]
            m_new = jnp.maximum(m_old, jnp.max(jnp.where(allowed, scores, NEG), axis=1, keepdims=True))
            weights = jnp.where(allowed, jnp.exp(scores - m_new), 0.0)
            factor = jnp.exp(m_old - m_new)
            l_ref[h] = l_ref[h] * factor + jnp.sum(weights, axis=1, keepdims=True)
            acc_ref[:, cols] = acc_ref[:, cols] * factor + jnp.dot(
                weights.astype(jnp.bfloat16), val_blk, preferred_element_type=jnp.float32
            )
            m_ref[h] = m_new
        return carry

    lax.fori_loop(lo, hi + 1, forward_block, 0)

    for h in range(heads):
        cols = slice(h * HD, (h + 1) * HD)
        attn = (acc_ref[:, cols] / l_ref[h]).astype(jnp.bfloat16)
        out_ref[:, cols] = attn
        lse_ref[h] = m_ref[h] + jnp.log(l_ref[h])
        dl_ref[h] = jnp.sum(
            g_ref[:, cols].astype(jnp.float32) * attn.astype(jnp.float32), axis=1, keepdims=True
        )
    dqa_ref[...] = jnp.zeros(dqa_ref.shape, jnp.float32)
    terms_ref[...] = jnp.zeros(terms_ref.shape, terms_ref.dtype)

    def backward_block(j, carry):
        key_blk, val_blk = key_value(j)
        allowed = allowed_of(j)
        dk = jnp.zeros((tokens, HD), jnp.float32)
        dv = jnp.zeros((tokens, HD), jnp.float32)
        for h in range(heads):
            cols = slice(h * HD, (h + 1) * HD)
            q_h = q_ref[:, cols]
            g_h = g_ref[:, cols]
            scores = (
                lax.dot_general(q_h, key_blk, contract_last, preferred_element_type=jnp.float32) * scale
            )
            probs = jnp.where(allowed, jnp.exp(scores - lse_ref[h]), 0.0)
            dv = dv + lax.dot_general(
                probs.astype(jnp.bfloat16), g_h, contract_first, preferred_element_type=jnp.float32
            )
            dprobs = lax.dot_general(g_h, val_blk, contract_last, preferred_element_type=jnp.float32)
            dscores = (probs * (dprobs - dl_ref[h])).astype(jnp.bfloat16)
            dqa_ref[:, cols] = dqa_ref[:, cols] + jnp.dot(
                dscores, key_blk, preferred_element_type=jnp.float32
            )
            dk = dk + lax.dot_general(dscores, q_h, contract_first, preferred_element_type=jnp.float32)
        terms_ref[hi - j, :, 0:HD] = (dk * scale).astype(terms_ref.dtype)
        terms_ref[hi - j, :, HD : 2 * HD] = dv.astype(terms_ref.dtype)
        return carry

    lax.fori_loop(lo, hi + 1, backward_block, 0)
    dq_ref[...] = (dqa_ref[...] * scale).astype(dq_ref.dtype)


def attention_local(bounds, q_loc, g_loc, kv_all, qpos, qstart, window):
    tokens, width = q_loc.shape
    heads = width // HD
    vmem = pl.BlockSpec(memory_space=pltpu.VMEM)
    return pl.pallas_call(
        attention_kernel,
        out_shape=(
            jax.ShapeDtypeStruct((tokens, width), jnp.bfloat16),
            jax.ShapeDtypeStruct((tokens, width), jnp.bfloat16),
            jax.ShapeDtypeStruct((window, tokens, 2 * HD), jnp.float32),
        ),
        in_specs=[pl.BlockSpec(memory_space=pltpu.SMEM)] + [vmem] * 5,
        out_specs=(vmem, vmem, vmem),
        scratch_shapes=[
            pltpu.VMEM((heads, tokens, 1), jnp.float32),
            pltpu.VMEM((heads, tokens, 1), jnp.float32),
            pltpu.VMEM((tokens, width), jnp.float32),
            pltpu.VMEM((heads, tokens, 1), jnp.float32),
            pltpu.VMEM((heads, tokens, 1), jnp.float32),
            pltpu.VMEM((tokens, width), jnp.float32),
        ],
    )(bounds, q_loc, g_loc, kv_all, qpos, qstart)


def window_stages(width):
    levels = max(1, (width - 1).bit_length())
    need = [None] * (levels + 1)
    need[levels] = [0]
    for k in reversed(range(levels)):
        step = 1 << k
        need[k] = sorted(set(need[k + 1]) | {e + step for e in need[k + 1] if e + step < width})
    return [[e for e in need[k + 1] if e + step < width] for k, step in enumerate(1 << k for k in range(levels))]


def reduce_kernel(stages, count, terms_ref, out_ref, held, *rest):
    depth = len(stages)
    send_bufs, recv_bufs = rest[:depth], rest[depth : 2 * depth]
    send_sem, recv_sem = rest[2 * depth], rest[2 * depth + 1]
    me = lax.axis_index("ctx")
    held[...] = terms_ref[...]
    for k, pairs in enumerate(stages):
        step = 1 << k
        copy = pltpu.make_async_remote_copy(
            src_ref=send_bufs[k],
            dst_ref=recv_bufs[k],
            send_sem=send_sem.at[k],
            recv_sem=recv_sem.at[k],
            device_id={"ctx": (me - step + count) % count},
            device_id_type=pl.DeviceIdType.MESH,
        )

        @pl.when(me >= step)
        def _():
            for i, e in enumerate(pairs):
                send_bufs[k][i] = held[e + step].astype(jnp.bfloat16)
            copy.start()

        @pl.when(me + step < count)
        def _():
            copy.wait_recv()
            for i, e in enumerate(pairs):
                held[e] = held[e] + recv_bufs[k][i].astype(jnp.float32)

        @pl.when(me >= step)
        def _():
            copy.wait_send()

    out_ref[...] = held[0]


def window_reduce(terms, axis):
    width, tokens, cols = terms.shape
    count = lax.axis_size(axis)
    stages = [pairs for k, pairs in enumerate(window_stages(width)) if (1 << k) < count]
    vmem = pl.BlockSpec(memory_space=pltpu.VMEM)
    bufs = [pltpu.VMEM((len(p), tokens, cols), jnp.bfloat16) for p in stages]
    return pl.pallas_call(
        functools.partial(reduce_kernel, stages, count),
        out_shape=jax.ShapeDtypeStruct((tokens, cols), jnp.float32),
        in_specs=[vmem],
        out_specs=vmem,
        scratch_shapes=[pltpu.VMEM((width, tokens, cols), jnp.float32)]
        + bufs
        + bufs
        + [pltpu.SemaphoreType.DMA((len(stages),)), pltpu.SemaphoreType.DMA((len(stages),))],
        compiler_params=pltpu.CompilerParams(has_side_effects=True),
    )(terms)


def body(
    record_lengths,
    query_heads,
    key_heads,
    value_heads,
    out_grad,
    gate_input,
    key_input,
    value_input,
    hyena_grad,
    short_filter,
    long_filter,
):
    tp = lax.axis_size("tp")
    rows = query_heads.shape[0]

    def exchange(pieces):
        widths = [x.shape[1] // tp for x in pieces]
        joined = jnp.concatenate([x.reshape(rows, tp, w) for x, w in zip(pieces, widths)], axis=2)
        joined = lax.all_to_all(joined, "tp", split_axis=1, concat_axis=0, tiled=True)
        return joined.reshape(rows * tp, sum(widths))

    kv_loc = exchange([key_heads, value_heads])
    kv_all = lax.all_gather(kv_loc, "ctx", axis=0, tiled=True)
    qg_loc = exchange([query_heads, out_grad])
    width = query_heads.shape[1] // tp
    q_loc, g_loc = qg_loc[:, :width], qg_loc[:, width:]
    tokens = q_loc.shape[0]
    ends = jnp.cumsum(record_lengths)
    starts = ends - record_lengths

    def start_of(positions):
        seg = jnp.sum((starts[None, :] <= positions[:, None]).astype(jnp.int32), axis=1) - 1
        return jnp.take(starts, seg)

    own = lax.axis_index("ctx")
    q_start = own * tokens
    q_pos = q_start + jnp.arange(tokens, dtype=jnp.int32)
    q_rec = start_of(q_pos)
    window = (MOST - 1) // tokens + 2
    first = jnp.maximum(q_rec[0] // tokens, own - (window - 1))
    bounds = jnp.stack([first, own]).astype(jnp.int32)
    attn_out, grad_query, terms = attention_local(
        bounds, q_loc, g_loc, kv_all, q_pos[:, None], q_rec[:, None], window
    )
    key_grads = window_reduce(terms, "ctx")
    grad_key = key_grads[:, :HD].astype(jnp.bfloat16)
    grad_value = key_grads[:, HD:].astype(jnp.bfloat16)
    streams = jnp.stack([gate_input, key_input, value_input, hyena_grad], axis=1)
    padded = padded_2(streams, (("ctx", 0),), HALO)
    hyena_val, grad_gate, grad_keyx, grad_valuex = hyena_local(
        padded, short_filter, long_filter, streams.shape[0]
    )
    return (
        attn_out,
        grad_query,
        grad_key,
        grad_value,
        hyena_val,
        grad_gate,
        grad_keyx,
        grad_valuex,
    )


def solution(mesh):
    placed = (
        P(),
        P(("ctx", "tp"), None),
        P(("ctx", "tp"), None),
        P(("ctx", "tp"), None),
        P(("ctx", "tp"), None),
        P("ctx", "tp"),
        P("ctx", "tp"),
        P("ctx", "tp"),
        P("ctx", "tp"),
        P(None, None, "tp"),
        P(None, "tp"),
    )
    return jax.shard_map(
        body,
        mesh=mesh,
        in_specs=placed,
        out_specs=(
            P("ctx", "tp"),
            P("ctx", "tp"),
            P("ctx", "tp"),
            P("ctx", "tp"),
            P("ctx", "tp"),
            P("ctx", "tp"),
            P("ctx", "tp"),
            P("ctx", "tp"),
        ),
        check_vma=False,
    )
```

```python
import functools

import jax
import jax.numpy as jnp
from jax import lax
from jax.experimental import pallas as pl
from jax.experimental.pallas import tpu as pltpu
from jax.sharding import PartitionSpec as P

HD = 128
QH = 64
KVH = 8
GROUP = 16
TAPS = 7
SHORT = 3
HALO = 8
MOST = 3264


NEG = -1e30


def padded_2(cells, sides, width):
    for axis, dim in sides:
        count = lax.axis_size(axis)
        ends = count - 1
        head = lax.slice_in_dim(cells, 0, width, axis=dim)
        tail = lax.slice_in_dim(cells, cells.shape[dim] - width, cells.shape[dim], axis=dim)
        cells = jnp.concatenate(
            [
                lax.ppermute(tail, axis, [(i, (i + 1) % count) for i in range(ends)]),
                cells,
                lax.ppermute(head, axis, [((i + 1) % count, i) for i in range(ends)]),
            ],
            axis=dim,
        )
    return cells


def hyena_local(padded, short_filter, long_filter, tokens):
    wide = padded.astype(jnp.float32)
    rows = wide.shape[0]
    lead = SHORT - 1
    per_channel = jnp.repeat(long_filter, GROUP, axis=1)

    def featurize(values, taps):
        result = taps[0] * values[lead:rows]
        for index in range(1, SHORT):
            result = result + taps[index] * values[lead - index : rows - index]
        return result

    gate_f = featurize(wide[:, 0], short_filter[0])
    key_f = featurize(wide[:, 1], short_filter[1])
    value_f = featurize(wide[:, 2], short_filter[2])
    mixed = key_f * value_f
    offset = HALO - lead
    span = rows - HALO
    conv = per_channel[0] * mixed[offset : offset + span]
    for index in range(1, TAPS):
        conv = conv + per_channel[index] * mixed[offset - index : offset - index + span]
    gate_c = gate_f[offset:]
    grad_c = wide[HALO:, 3]
    hyena_val = (gate_c[:tokens] * conv[:tokens]).astype(jnp.bfloat16)
    dconv = grad_c * gate_c
    dgate_f = grad_c * conv
    dmixed = per_channel[0] * dconv[0 : tokens + lead]
    for index in range(1, TAPS):
        dmixed = dmixed + per_channel[index] * dconv[index : index + tokens + lead]
    key_c = key_f[offset : offset + tokens + lead]
    value_c = value_f[offset : offset + tokens + lead]
    dkey_f = dmixed * value_c
    dvalue_f = dmixed * key_c

    def unfeaturize(grads, taps):
        result = taps[0] * grads[0:tokens]
        for index in range(1, SHORT):
            result = result + taps[index] * grads[index : index + tokens]
        return result.astype(jnp.bfloat16)

    return (
        hyena_val,
        unfeaturize(dgate_f, short_filter[0]),
        unfeaturize(dkey_f, short_filter[1]),
        unfeaturize(dvalue_f, short_filter[2]),
    )


def attention_kernel(
    bounds_ref, q_ref, g_ref, kv_ref, qpos_ref, qstart_ref,
    out_ref, dq_ref, terms_ref,
    qs_ref, gs_ref, m_ref, l_ref, acc_ref, lse_ref, dl_ref, dqa_ref,
):
    tokens = q_ref.shape[0]
    heads = q_ref.shape[1] // HD
    scale = HD ** (-0.5)
    lo = bounds_ref[0]
    hi = bounds_ref[1]
    qpos = qpos_ref[...]
    qstart = qstart_ref[...]
    contract_last = (((1,), (1,)), ((), ()))
    contract_first = (((0,), (0,)), ((), ()))
    for h in range(heads):
        qs_ref[h * tokens : (h + 1) * tokens, :] = q_ref[:, h * HD : (h + 1) * HD]
        gs_ref[h * tokens : (h + 1) * tokens, :] = g_ref[:, h * HD : (h + 1) * HD]

    def allowed_of(j):
        kpos = j * tokens + lax.broadcasted_iota(jnp.int32, (1, tokens), 1)
        return (kpos <= qpos) & (kpos >= qstart)

    def key_value(j):
        rows = pl.ds(pl.multiple_of(j * tokens, 64), tokens)
        return kv_ref[rows, 0:HD], kv_ref[rows, HD : 2 * HD]

    m_ref[...] = jnp.full(m_ref.shape, NEG, jnp.float32)
    l_ref[...] = jnp.zeros(l_ref.shape, jnp.float32)
    acc_ref[...] = jnp.zeros(acc_ref.shape, jnp.float32)

    def forward_block(j, carry):
        key_blk, val_blk = key_value(j)
        allowed = allowed_of(j)
        scores = (
            lax.dot_general(qs_ref[...], key_blk, contract_last, preferred_element_type=jnp.float32)
            * scale
        )
        m_old = m_ref[...]
        m_new = jnp.maximum(m_old, jnp.max(jnp.where(allowed, scores, NEG), axis=1, keepdims=True))
        weights = jnp.where(allowed, jnp.exp(scores - m_new), 0.0)
        factor = jnp.exp(m_old - m_new)
        l_ref[...] = l_ref[...] * factor + jnp.sum(weights, axis=1, keepdims=True)
        acc_ref[...] = acc_ref[...] * factor + jnp.dot(
            weights.astype(jnp.bfloat16), val_blk, preferred_element_type=jnp.float32
        )
        m_ref[...] = m_new
        return carry

    lax.fori_loop(lo, hi + 1, forward_block, 0)

    attn = (acc_ref[...] / l_ref[...]).astype(jnp.bfloat16)
    lse_ref[...] = m_ref[...] + jnp.log(l_ref[...])
    dl_ref[...] = jnp.sum(gs_ref[...].astype(jnp.float32) * attn.astype(jnp.float32), axis=1, keepdims=True)
    for h in range(heads):
        out_ref[:, h * HD : (h + 1) * HD] = attn[h * tokens : (h + 1) * tokens]
    dqa_ref[...] = jnp.zeros(dqa_ref.shape, jnp.float32)
    terms_ref[...] = jnp.zeros(terms_ref.shape, terms_ref.dtype)

    def backward_block(j, carry):
        key_blk, val_blk = key_value(j)
        allowed = allowed_of(j)
        q_all = qs_ref[...]
        g_all = gs_ref[...]
        scores = lax.dot_general(q_all, key_blk, contract_last, preferred_element_type=jnp.float32) * scale
        probs = jnp.where(allowed, jnp.exp(scores - lse_ref[...]), 0.0)
        dv = lax.dot_general(
            probs.astype(jnp.bfloat16), g_all, contract_first, preferred_element_type=jnp.float32
        )
        dprobs = lax.dot_general(g_all, val_blk, contract_last, preferred_element_type=jnp.float32)
        dscores = (probs * (dprobs - dl_ref[...])).astype(jnp.bfloat16)
        dqa_ref[...] = dqa_ref[...] + jnp.dot(dscores, key_blk, preferred_element_type=jnp.float32)
        dk = lax.dot_general(dscores, q_all, contract_first, preferred_element_type=jnp.float32)
        terms_ref[hi - j, :, 0:HD] = (dk * scale).astype(terms_ref.dtype)
        terms_ref[hi - j, :, HD : 2 * HD] = dv.astype(terms_ref.dtype)
        return carry

    lax.fori_loop(lo, hi + 1, backward_block, 0)
    for h in range(heads):
        dq_ref[:, h * HD : (h + 1) * HD] = (
            dqa_ref[h * tokens : (h + 1) * tokens, :] * scale
        ).astype(dq_ref.dtype)


def attention_local(bounds, q_loc, g_loc, kv_all, qpos, qstart, window):
    tokens, width = q_loc.shape
    heads = width // HD
    rows = heads * tokens
    vmem = pl.BlockSpec(memory_space=pltpu.VMEM)
    return pl.pallas_call(
        attention_kernel,
        out_shape=(
            jax.ShapeDtypeStruct((tokens, width), jnp.bfloat16),
            jax.ShapeDtypeStruct((tokens, width), jnp.bfloat16),
            jax.ShapeDtypeStruct((window, tokens, 2 * HD), jnp.float32),
        ),
        in_specs=[pl.BlockSpec(memory_space=pltpu.SMEM)] + [vmem] * 5,
        out_specs=(vmem, vmem, vmem),
        scratch_shapes=[
            pltpu.VMEM((rows, HD), jnp.bfloat16),
            pltpu.VMEM((rows, HD), jnp.bfloat16),
            pltpu.VMEM((rows, 1), jnp.float32),
            pltpu.VMEM((rows, 1), jnp.float32),
            pltpu.VMEM((rows, HD), jnp.float32),
            pltpu.VMEM((rows, 1), jnp.float32),
            pltpu.VMEM((rows, 1), jnp.float32),
            pltpu.VMEM((rows, HD), jnp.float32),
        ],
    )(bounds, q_loc, g_loc, kv_all, jnp.tile(qpos, (heads, 1)), jnp.tile(qstart, (heads, 1)))


def window_stages(width):
    levels = max(1, (width - 1).bit_length())
    need = [None] * (levels + 1)
    need[levels] = [0]
    for k in reversed(range(levels)):
        step = 1 << k
        need[k] = sorted(set(need[k + 1]) | {e + step for e in need[k + 1] if e + step < width})
    return [[e for e in need[k + 1] if e + step < width] for k, step in enumerate(1 << k for k in range(levels))]


def reduce_kernel(stages, count, terms_ref, out_ref, held, *rest):
    depth = len(stages)
    send_bufs, recv_bufs = rest[:depth], rest[depth : 2 * depth]
    send_sem, recv_sem = rest[2 * depth], rest[2 * depth + 1]
    me = lax.axis_index("ctx")
    held[...] = terms_ref[...]
    for k, pairs in enumerate(stages):
        step = 1 << k
        copy = pltpu.make_async_remote_copy(
            src_ref=send_bufs[k],
            dst_ref=recv_bufs[k],
            send_sem=send_sem.at[k],
            recv_sem=recv_sem.at[k],
            device_id={"ctx": (me - step + count) % count},
            device_id_type=pl.DeviceIdType.MESH,
        )

        @pl.when(me >= step)
        def _():
            for i, e in enumerate(pairs):
                send_bufs[k][i] = held[e + step].astype(jnp.bfloat16)
            copy.start()

        @pl.when(me + step < count)
        def _():
            copy.wait_recv()
            for i, e in enumerate(pairs):
                held[e] = held[e] + recv_bufs[k][i].astype(jnp.float32)

        @pl.when(me >= step)
        def _():
            copy.wait_send()

    out_ref[...] = held[0]


def window_reduce(terms, axis):
    width, tokens, cols = terms.shape
    count = lax.axis_size(axis)
    stages = [pairs for k, pairs in enumerate(window_stages(width)) if (1 << k) < count]
    vmem = pl.BlockSpec(memory_space=pltpu.VMEM)
    bufs = [pltpu.VMEM((len(p), tokens, cols), jnp.bfloat16) for p in stages]
    return pl.pallas_call(
        functools.partial(reduce_kernel, stages, count),
        out_shape=jax.ShapeDtypeStruct((tokens, cols), jnp.float32),
        in_specs=[vmem],
        out_specs=vmem,
        scratch_shapes=[pltpu.VMEM((width, tokens, cols), jnp.float32)]
        + bufs
        + bufs
        + [pltpu.SemaphoreType.DMA((len(stages),)), pltpu.SemaphoreType.DMA((len(stages),))],
        compiler_params=pltpu.CompilerParams(has_side_effects=True),
    )(terms)


def body(
    record_lengths,
    query_heads,
    key_heads,
    value_heads,
    out_grad,
    gate_input,
    key_input,
    value_input,
    hyena_grad,
    short_filter,
    long_filter,
):
    tp = lax.axis_size("tp")
    rows = query_heads.shape[0]

    def exchange(pieces):
        widths = [x.shape[1] // tp for x in pieces]
        joined = jnp.concatenate([x.reshape(rows, tp, w) for x, w in zip(pieces, widths)], axis=2)
        joined = lax.all_to_all(joined, "tp", split_axis=1, concat_axis=0, tiled=True)
        return joined.reshape(rows * tp, sum(widths))

    kv_loc = exchange([key_heads, value_heads])
    kv_all = lax.all_gather(kv_loc, "ctx", axis=0, tiled=True)
    qg_loc = exchange([query_heads, out_grad])
    width = query_heads.shape[1] // tp
    q_loc, g_loc = qg_loc[:, :width], qg_loc[:, width:]
    tokens = q_loc.shape[0]
    ends = jnp.cumsum(record_lengths)
    starts = ends - record_lengths

    def start_of(positions):
        seg = jnp.sum((starts[None, :] <= positions[:, None]).astype(jnp.int32), axis=1) - 1
        return jnp.take(starts, seg)

    own = lax.axis_index("ctx")
    q_start = own * tokens
    q_pos = q_start + jnp.arange(tokens, dtype=jnp.int32)
    q_rec = start_of(q_pos)
    window = (MOST - 1) // tokens + 2
    first = jnp.maximum(q_rec[0] // tokens, own - (window - 1))
    bounds = jnp.stack([first, own]).astype(jnp.int32)
    attn_out, grad_query, terms = attention_local(
        bounds, q_loc, g_loc, kv_all, q_pos[:, None], q_rec[:, None], window
    )
    key_grads = window_reduce(terms, "ctx")
    grad_key = key_grads[:, :HD].astype(jnp.bfloat16)
    grad_value = key_grads[:, HD:].astype(jnp.bfloat16)
    streams = jnp.stack([gate_input, key_input, value_input, hyena_grad], axis=1)
    padded = padded_2(streams, (("ctx", 0),), HALO)
    hyena_val, grad_gate, grad_keyx, grad_valuex = hyena_local(
        padded, short_filter, long_filter, streams.shape[0]
    )
    return (
        attn_out,
        grad_query,
        grad_key,
        grad_value,
        hyena_val,
        grad_gate,
        grad_keyx,
        grad_valuex,
    )


def solution(mesh):
    placed = (
        P(),
        P(("ctx", "tp"), None),
        P(("ctx", "tp"), None),
        P(("ctx", "tp"), None),
        P(("ctx", "tp"), None),
        P("ctx", "tp"),
        P("ctx", "tp"),
        P("ctx", "tp"),
        P("ctx", "tp"),
        P(None, None, "tp"),
        P(None, "tp"),
    )
    return jax.shard_map(
        body,
        mesh=mesh,
        in_specs=placed,
        out_specs=(
            P("ctx", "tp"),
            P("ctx", "tp"),
            P("ctx", "tp"),
            P("ctx", "tp"),
            P("ctx", "tp"),
            P("ctx", "tp"),
            P("ctx", "tp"),
            P("ctx", "tp"),
        ),
        check_vma=False,
    )
```

```python
import functools

import jax
import jax.numpy as jnp
from jax import lax
from jax.experimental import pallas as pl
from jax.experimental.pallas import tpu as pltpu
from jax.sharding import PartitionSpec as P

HD = 128
QH = 64
KVH = 8
GROUP = 16
TAPS = 7
SHORT = 3
HALO = 8
MOST = 3264


NEG = -1e30


def padded_2(cells, sides, width):
    for axis, dim in sides:
        count = lax.axis_size(axis)
        ends = count - 1
        head = lax.slice_in_dim(cells, 0, width, axis=dim)
        tail = lax.slice_in_dim(cells, cells.shape[dim] - width, cells.shape[dim], axis=dim)
        cells = jnp.concatenate(
            [
                lax.ppermute(tail, axis, [(i, (i + 1) % count) for i in range(ends)]),
                cells,
                lax.ppermute(head, axis, [((i + 1) % count, i) for i in range(ends)]),
            ],
            axis=dim,
        )
    return cells


def hyena_local(padded, short_filter, long_filter, tokens):
    wide = padded.astype(jnp.float32)
    rows = wide.shape[0]
    lead = SHORT - 1
    per_channel = jnp.repeat(long_filter, GROUP, axis=1)

    def featurize(values, taps):
        result = taps[0] * values[lead:rows]
        for index in range(1, SHORT):
            result = result + taps[index] * values[lead - index : rows - index]
        return result

    gate_f = featurize(wide[:, 0], short_filter[0])
    key_f = featurize(wide[:, 1], short_filter[1])
    value_f = featurize(wide[:, 2], short_filter[2])
    mixed = key_f * value_f
    offset = HALO - lead
    span = rows - HALO
    conv = per_channel[0] * mixed[offset : offset + span]
    for index in range(1, TAPS):
        conv = conv + per_channel[index] * mixed[offset - index : offset - index + span]
    gate_c = gate_f[offset:]
    grad_c = wide[HALO:, 3]
    hyena_val = (gate_c[:tokens] * conv[:tokens]).astype(jnp.bfloat16)
    dconv = grad_c * gate_c
    dgate_f = grad_c * conv
    dmixed = per_channel[0] * dconv[0 : tokens + lead]
    for index in range(1, TAPS):
        dmixed = dmixed + per_channel[index] * dconv[index : index + tokens + lead]
    key_c = key_f[offset : offset + tokens + lead]
    value_c = value_f[offset : offset + tokens + lead]
    dkey_f = dmixed * value_c
    dvalue_f = dmixed * key_c

    def unfeaturize(grads, taps):
        result = taps[0] * grads[0:tokens]
        for index in range(1, SHORT):
            result = result + taps[index] * grads[index : index + tokens]
        return result.astype(jnp.bfloat16)

    return (
        hyena_val,
        unfeaturize(dgate_f, short_filter[0]),
        unfeaturize(dkey_f, short_filter[1]),
        unfeaturize(dvalue_f, short_filter[2]),
    )


def attention_kernel(
    bounds_ref, q_ref, g_ref, kv_ref, qpos_ref, qstart_ref, qt_ref, gt_ref,
    out_ref, dq_ref, terms_ref,
    qs_ref, gs_ref, m_ref, l_ref, acc_ref, lse_ref, dl_ref, dqa_ref,
):
    tokens = q_ref.shape[0]
    heads = q_ref.shape[1] // HD
    scale = HD ** (-0.5)
    lo = bounds_ref[0]
    hi = bounds_ref[1]
    qpos = qpos_ref[...]
    qstart = qstart_ref[...]
    contract_last = (((1,), (1,)), ((), ()))
    for h in range(heads):
        qs_ref[h * tokens : (h + 1) * tokens, :] = q_ref[:, h * HD : (h + 1) * HD]
        gs_ref[h * tokens : (h + 1) * tokens, :] = g_ref[:, h * HD : (h + 1) * HD]

    def allowed_of(j):
        kpos = j * tokens + lax.broadcasted_iota(jnp.int32, (1, tokens), 1)
        return (kpos <= qpos) & (kpos >= qstart)

    def key_value(j):
        rows = pl.ds(pl.multiple_of(j * tokens, 64), tokens)
        return kv_ref[rows, 0:HD], kv_ref[rows, HD : 2 * HD]

    m_ref[...] = jnp.full(m_ref.shape, NEG, jnp.float32)
    l_ref[...] = jnp.zeros(l_ref.shape, jnp.float32)
    acc_ref[...] = jnp.zeros(acc_ref.shape, jnp.float32)

    def forward_block(j, carry):
        key_blk, val_blk = key_value(j)
        allowed = allowed_of(j)
        scores = (
            lax.dot_general(qs_ref[...], key_blk, contract_last, preferred_element_type=jnp.float32)
            * scale
        )
        m_old = m_ref[...]
        m_new = jnp.maximum(m_old, jnp.max(jnp.where(allowed, scores, NEG), axis=1, keepdims=True))
        weights = jnp.where(allowed, jnp.exp(scores - m_new), 0.0)
        factor = jnp.exp(m_old - m_new)
        l_ref[...] = l_ref[...] * factor + jnp.sum(weights, axis=1, keepdims=True)
        acc_ref[...] = acc_ref[...] * factor + jnp.dot(
            weights.astype(jnp.bfloat16), val_blk, preferred_element_type=jnp.float32
        )
        m_ref[...] = m_new
        return carry

    lax.fori_loop(lo, hi + 1, forward_block, 0)

    attn = (acc_ref[...] / l_ref[...]).astype(jnp.bfloat16)
    lse_ref[...] = m_ref[...] + jnp.log(l_ref[...])
    dl_ref[...] = jnp.sum(gs_ref[...].astype(jnp.float32) * attn.astype(jnp.float32), axis=1, keepdims=True)
    for h in range(heads):
        out_ref[:, h * HD : (h + 1) * HD] = attn[h * tokens : (h + 1) * tokens]
    dqa_ref[...] = jnp.zeros(dqa_ref.shape, jnp.float32)
    terms_ref[...] = jnp.zeros(terms_ref.shape, terms_ref.dtype)

    def backward_block(j, carry):
        key_blk, val_blk = key_value(j)
        allowed = allowed_of(j)
        q_all = qs_ref[...]
        g_all = gs_ref[...]
        scores = lax.dot_general(q_all, key_blk, contract_last, preferred_element_type=jnp.float32) * scale
        probs = jnp.where(allowed, jnp.exp(scores - lse_ref[...]), 0.0)
        dv_t = jnp.dot(gt_ref[...], probs.astype(jnp.bfloat16), preferred_element_type=jnp.float32)
        dprobs = lax.dot_general(g_all, val_blk, contract_last, preferred_element_type=jnp.float32)
        dscores = (probs * (dprobs - dl_ref[...])).astype(jnp.bfloat16)
        dqa_ref[...] = dqa_ref[...] + jnp.dot(dscores, key_blk, preferred_element_type=jnp.float32)
        dk_t = jnp.dot(qt_ref[...], dscores, preferred_element_type=jnp.float32)
        terms_ref[hi - j, 0:HD, :] = (dk_t * scale).astype(terms_ref.dtype)
        terms_ref[hi - j, HD : 2 * HD, :] = dv_t.astype(terms_ref.dtype)
        return carry

    lax.fori_loop(lo, hi + 1, backward_block, 0)
    for h in range(heads):
        dq_ref[:, h * HD : (h + 1) * HD] = (
            dqa_ref[h * tokens : (h + 1) * tokens, :] * scale
        ).astype(dq_ref.dtype)


def attention_local(bounds, q_loc, g_loc, kv_all, qpos, qstart, window):
    tokens, width = q_loc.shape
    heads = width // HD
    rows = heads * tokens
    vmem = pl.BlockSpec(memory_space=pltpu.VMEM)
    return pl.pallas_call(
        attention_kernel,
        out_shape=(
            jax.ShapeDtypeStruct((tokens, width), jnp.bfloat16),
            jax.ShapeDtypeStruct((tokens, width), jnp.bfloat16),
            jax.ShapeDtypeStruct((window, 2 * HD, tokens), jnp.float32),
        ),
        in_specs=[pl.BlockSpec(memory_space=pltpu.SMEM)] + [vmem] * 7,
        out_specs=(vmem, vmem, vmem),
        scratch_shapes=[
            pltpu.VMEM((rows, HD), jnp.bfloat16),
            pltpu.VMEM((rows, HD), jnp.bfloat16),
            pltpu.VMEM((rows, 1), jnp.float32),
            pltpu.VMEM((rows, 1), jnp.float32),
            pltpu.VMEM((rows, HD), jnp.float32),
            pltpu.VMEM((rows, 1), jnp.float32),
            pltpu.VMEM((rows, 1), jnp.float32),
            pltpu.VMEM((rows, HD), jnp.float32),
        ],
    )(
        bounds, q_loc, g_loc, kv_all, jnp.tile(qpos, (heads, 1)), jnp.tile(qstart, (heads, 1)),
        heads_major_t(q_loc), heads_major_t(g_loc),
    )


def heads_major_t(x):
    tokens, width = x.shape
    return x.reshape(tokens, width // HD, HD).transpose(2, 1, 0).reshape(HD, width // HD * tokens)


def window_stages(width):
    levels = max(1, (width - 1).bit_length())
    need = [None] * (levels + 1)
    need[levels] = [0]
    for k in reversed(range(levels)):
        step = 1 << k
        need[k] = sorted(set(need[k + 1]) | {e + step for e in need[k + 1] if e + step < width})
    return [[e for e in need[k + 1] if e + step < width] for k, step in enumerate(1 << k for k in range(levels))]


def reduce_kernel(stages, count, terms_ref, out_ref, held, *rest):
    depth = len(stages)
    send_bufs, recv_bufs = rest[:depth], rest[depth : 2 * depth]
    send_sem, recv_sem = rest[2 * depth], rest[2 * depth + 1]
    me = lax.axis_index("ctx")
    held[...] = terms_ref[...]
    for k, pairs in enumerate(stages):
        step = 1 << k
        copy = pltpu.make_async_remote_copy(
            src_ref=send_bufs[k],
            dst_ref=recv_bufs[k],
            send_sem=send_sem.at[k],
            recv_sem=recv_sem.at[k],
            device_id={"ctx": (me - step + count) % count},
            device_id_type=pl.DeviceIdType.MESH,
        )

        @pl.when(me >= step)
        def _():
            for i, e in enumerate(pairs):
                send_bufs[k][i] = held[e + step].astype(jnp.bfloat16)
            copy.start()

        @pl.when(me + step < count)
        def _():
            copy.wait_recv()
            for i, e in enumerate(pairs):
                held[e] = held[e] + recv_bufs[k][i].astype(jnp.float32)

        @pl.when(me >= step)
        def _():
            copy.wait_send()

    out_ref[...] = held[0]


def window_reduce(terms, axis):
    width, tokens, cols = terms.shape
    count = lax.axis_size(axis)
    stages = [pairs for k, pairs in enumerate(window_stages(width)) if (1 << k) < count]
    vmem = pl.BlockSpec(memory_space=pltpu.VMEM)
    bufs = [pltpu.VMEM((len(p), tokens, cols), jnp.bfloat16) for p in stages]
    return pl.pallas_call(
        functools.partial(reduce_kernel, stages, count),
        out_shape=jax.ShapeDtypeStruct((tokens, cols), jnp.float32),
        in_specs=[vmem],
        out_specs=vmem,
        scratch_shapes=[pltpu.VMEM((width, tokens, cols), jnp.float32)]
        + bufs
        + bufs
        + [pltpu.SemaphoreType.DMA((len(stages),)), pltpu.SemaphoreType.DMA((len(stages),))],
        compiler_params=pltpu.CompilerParams(has_side_effects=True),
    )(terms)


def body(
    record_lengths,
    query_heads,
    key_heads,
    value_heads,
    out_grad,
    gate_input,
    key_input,
    value_input,
    hyena_grad,
    short_filter,
    long_filter,
):
    tp = lax.axis_size("tp")
    rows = query_heads.shape[0]

    def exchange(pieces):
        widths = [x.shape[1] // tp for x in pieces]
        joined = jnp.concatenate([x.reshape(rows, tp, w) for x, w in zip(pieces, widths)], axis=2)
        joined = lax.all_to_all(joined, "tp", split_axis=1, concat_axis=0, tiled=True)
        return joined.reshape(rows * tp, sum(widths))

    kv_loc = exchange([key_heads, value_heads])
    kv_all = lax.all_gather(kv_loc, "ctx", axis=0, tiled=True)
    qg_loc = exchange([query_heads, out_grad])
    width = query_heads.shape[1] // tp
    q_loc, g_loc = qg_loc[:, :width], qg_loc[:, width:]
    tokens = q_loc.shape[0]
    ends = jnp.cumsum(record_lengths)
    starts = ends - record_lengths

    def start_of(positions):
        seg = jnp.sum((starts[None, :] <= positions[:, None]).astype(jnp.int32), axis=1) - 1
        return jnp.take(starts, seg)

    own = lax.axis_index("ctx")
    q_start = own * tokens
    q_pos = q_start + jnp.arange(tokens, dtype=jnp.int32)
    q_rec = start_of(q_pos)
    window = (MOST - 1) // tokens + 2
    first = jnp.maximum(q_rec[0] // tokens, own - (window - 1))
    bounds = jnp.stack([first, own]).astype(jnp.int32)
    attn_out, grad_query, terms = attention_local(
        bounds, q_loc, g_loc, kv_all, q_pos[:, None], q_rec[:, None], window
    )
    key_grads = window_reduce(terms, "ctx")
    grad_key = key_grads[:HD].T.astype(jnp.bfloat16)
    grad_value = key_grads[HD:].T.astype(jnp.bfloat16)
    streams = jnp.stack([gate_input, key_input, value_input, hyena_grad], axis=1)
    padded = padded_2(streams, (("ctx", 0),), HALO)
    hyena_val, grad_gate, grad_keyx, grad_valuex = hyena_local(
        padded, short_filter, long_filter, streams.shape[0]
    )
    return (
        attn_out,
        grad_query,
        grad_key,
        grad_value,
        hyena_val,
        grad_gate,
        grad_keyx,
        grad_valuex,
    )


def solution(mesh):
    placed = (
        P(),
        P(("ctx", "tp"), None),
        P(("ctx", "tp"), None),
        P(("ctx", "tp"), None),
        P(("ctx", "tp"), None),
        P("ctx", "tp"),
        P("ctx", "tp"),
        P("ctx", "tp"),
        P("ctx", "tp"),
        P(None, None, "tp"),
        P(None, "tp"),
    )
    return jax.shard_map(
        body,
        mesh=mesh,
        in_specs=placed,
        out_specs=(
            P("ctx", "tp"),
            P("ctx", "tp"),
            P("ctx", "tp"),
            P("ctx", "tp"),
            P("ctx", "tp"),
            P("ctx", "tp"),
            P("ctx", "tp"),
            P("ctx", "tp"),
        ),
        check_vma=False,
    )
```

```python
import functools

import jax
import jax.numpy as jnp
from jax import lax
from jax.experimental import pallas as pl
from jax.experimental.pallas import tpu as pltpu
from jax.sharding import PartitionSpec as P

HD = 128
QH = 64
KVH = 8
GROUP = 16
TAPS = 7
SHORT = 3
HALO = 8
MOST = 3264


NEG = -1e30


def padded_2(cells, sides, width):
    for axis, dim in sides:
        count = lax.axis_size(axis)
        ends = count - 1
        head = lax.slice_in_dim(cells, 0, width, axis=dim)
        tail = lax.slice_in_dim(cells, cells.shape[dim] - width, cells.shape[dim], axis=dim)
        cells = jnp.concatenate(
            [
                lax.ppermute(tail, axis, [(i, (i + 1) % count) for i in range(ends)]),
                cells,
                lax.ppermute(head, axis, [((i + 1) % count, i) for i in range(ends)]),
            ],
            axis=dim,
        )
    return cells


def hyena_local(padded, short_filter, long_filter, tokens):
    wide = padded.astype(jnp.float32)
    rows = wide.shape[0]
    lead = SHORT - 1
    per_channel = jnp.repeat(long_filter, GROUP, axis=1)

    def featurize(values, taps):
        result = taps[0] * values[lead:rows]
        for index in range(1, SHORT):
            result = result + taps[index] * values[lead - index : rows - index]
        return result

    gate_f = featurize(wide[:, 0], short_filter[0])
    key_f = featurize(wide[:, 1], short_filter[1])
    value_f = featurize(wide[:, 2], short_filter[2])
    mixed = key_f * value_f
    offset = HALO - lead
    span = rows - HALO
    conv = per_channel[0] * mixed[offset : offset + span]
    for index in range(1, TAPS):
        conv = conv + per_channel[index] * mixed[offset - index : offset - index + span]
    gate_c = gate_f[offset:]
    grad_c = wide[HALO:, 3]
    hyena_val = (gate_c[:tokens] * conv[:tokens]).astype(jnp.bfloat16)
    dconv = grad_c * gate_c
    dgate_f = grad_c * conv
    dmixed = per_channel[0] * dconv[0 : tokens + lead]
    for index in range(1, TAPS):
        dmixed = dmixed + per_channel[index] * dconv[index : index + tokens + lead]
    key_c = key_f[offset : offset + tokens + lead]
    value_c = value_f[offset : offset + tokens + lead]
    dkey_f = dmixed * value_c
    dvalue_f = dmixed * key_c

    def unfeaturize(grads, taps):
        result = taps[0] * grads[0:tokens]
        for index in range(1, SHORT):
            result = result + taps[index] * grads[index : index + tokens]
        return result.astype(jnp.bfloat16)

    return (
        hyena_val,
        unfeaturize(dgate_f, short_filter[0]),
        unfeaturize(dkey_f, short_filter[1]),
        unfeaturize(dvalue_f, short_filter[2]),
    )


def attention_kernel(
    bounds_ref, q_ref, g_ref, kv_ref, qpos_ref, qstart_ref, qt_ref, gt_ref,
    out_ref, dq_ref, terms_ref,
    qs_ref, gs_ref, m_ref, l_ref, acc_ref, lse_ref, dl_ref, dqa_ref,
):
    tokens = q_ref.shape[0]
    heads = q_ref.shape[1] // HD
    scale = HD ** (-0.5)
    lo = bounds_ref[0]
    hi = bounds_ref[1]
    qpos = qpos_ref[...]
    qstart = qstart_ref[...]
    contract_last = (((1,), (1,)), ((), ()))
    for h in range(heads):
        qs_ref[h * tokens : (h + 1) * tokens, :] = q_ref[:, h * HD : (h + 1) * HD]
        gs_ref[h * tokens : (h + 1) * tokens, :] = g_ref[:, h * HD : (h + 1) * HD]

    def allowed_of(j):
        kpos = j * tokens + lax.broadcasted_iota(jnp.int32, (1, tokens), 1)
        return (kpos <= qpos) & (kpos >= qstart)

    def key_value(j):
        rows = pl.ds(pl.multiple_of(j * tokens, 64), tokens)
        return kv_ref[rows, 0:HD], kv_ref[rows, HD : 2 * HD]

    m_ref[...] = jnp.full(m_ref.shape, NEG, jnp.float32)
    l_ref[...] = jnp.zeros(l_ref.shape, jnp.float32)
    acc_ref[...] = jnp.zeros(acc_ref.shape, jnp.float32)

    def forward_block(j, carry):
        key_blk, val_blk = key_value(j)
        allowed = allowed_of(j)
        scores = (
            lax.dot_general(qs_ref[...], key_blk, contract_last, preferred_element_type=jnp.float32)
            * scale
        )
        m_old = m_ref[...]
        m_new = jnp.maximum(m_old, jnp.max(jnp.where(allowed, scores, NEG), axis=1, keepdims=True))
        weights = jnp.where(allowed, jnp.exp(scores - m_new), 0.0)
        factor = jnp.exp(m_old - m_new)
        l_ref[...] = l_ref[...] * factor + jnp.sum(weights, axis=1, keepdims=True)
        acc_ref[...] = acc_ref[...] * factor + jnp.dot(
            weights.astype(jnp.bfloat16), val_blk, preferred_element_type=jnp.float32
        )
        m_ref[...] = m_new
        return carry

    lax.fori_loop(lo, hi + 1, forward_block, 0)

    attn = (acc_ref[...] / l_ref[...]).astype(jnp.bfloat16)
    lse_ref[...] = m_ref[...] + jnp.log(l_ref[...])
    dl_ref[...] = jnp.sum(gs_ref[...].astype(jnp.float32) * attn.astype(jnp.float32), axis=1, keepdims=True)
    for h in range(heads):
        out_ref[:, h * HD : (h + 1) * HD] = attn[h * tokens : (h + 1) * tokens]
    dqa_ref[...] = jnp.zeros(dqa_ref.shape, jnp.float32)
    terms_ref[...] = jnp.zeros(terms_ref.shape, terms_ref.dtype)

    def backward_block(j, carry):
        key_blk, val_blk = key_value(j)
        allowed = allowed_of(j)
        q_all = qs_ref[...]
        g_all = gs_ref[...]
        scores = lax.dot_general(q_all, key_blk, contract_last, preferred_element_type=jnp.float32) * scale
        probs = jnp.where(allowed, jnp.exp(scores - lse_ref[...]), 0.0)
        dv_t = jnp.dot(gt_ref[...], probs.astype(jnp.bfloat16), preferred_element_type=jnp.float32)
        dprobs = lax.dot_general(g_all, val_blk, contract_last, preferred_element_type=jnp.float32)
        dscores = (probs * (dprobs - dl_ref[...])).astype(jnp.bfloat16)
        dqa_ref[...] = dqa_ref[...] + jnp.dot(dscores, key_blk, preferred_element_type=jnp.float32)
        dk_t = jnp.dot(qt_ref[...], dscores, preferred_element_type=jnp.float32)
        terms_ref[hi - j, 0:HD, :] = (dk_t * scale).astype(terms_ref.dtype)
        terms_ref[hi - j, HD : 2 * HD, :] = dv_t.astype(terms_ref.dtype)
        return carry

    lax.fori_loop(lo, hi + 1, backward_block, 0)
    for h in range(heads):
        dq_ref[:, h * HD : (h + 1) * HD] = (
            dqa_ref[h * tokens : (h + 1) * tokens, :] * scale
        ).astype(dq_ref.dtype)


def attention_local(bounds, q_loc, g_loc, kv_all, qpos, qstart, window):
    tokens, width = q_loc.shape
    heads = width // HD
    rows = heads * tokens
    vmem = pl.BlockSpec(memory_space=pltpu.VMEM)
    return pl.pallas_call(
        attention_kernel,
        out_shape=(
            jax.ShapeDtypeStruct((tokens, width), jnp.bfloat16),
            jax.ShapeDtypeStruct((tokens, width), jnp.bfloat16),
            jax.ShapeDtypeStruct((window, 2 * HD, tokens), jnp.float32),
        ),
        in_specs=[pl.BlockSpec(memory_space=pltpu.SMEM)] + [vmem] * 7,
        out_specs=(vmem, vmem, vmem),
        scratch_shapes=[
            pltpu.VMEM((rows, HD), jnp.bfloat16),
            pltpu.VMEM((rows, HD), jnp.bfloat16),
            pltpu.VMEM((rows, 1), jnp.float32),
            pltpu.VMEM((rows, 1), jnp.float32),
            pltpu.VMEM((rows, HD), jnp.float32),
            pltpu.VMEM((rows, 1), jnp.float32),
            pltpu.VMEM((rows, 1), jnp.float32),
            pltpu.VMEM((rows, HD), jnp.float32),
        ],
    )(
        bounds, q_loc, g_loc, kv_all, jnp.tile(qpos, (heads, 1)), jnp.tile(qstart, (heads, 1)),
        heads_major_t(q_loc), heads_major_t(g_loc),
    )


def heads_major_t(x):
    tokens, width = x.shape
    return x.reshape(tokens, width // HD, HD).transpose(2, 1, 0).reshape(HD, width // HD * tokens)


def window_stages(width):
    levels = max(1, (width - 1).bit_length())
    need = [None] * (levels + 1)
    need[levels] = [0]
    for k in reversed(range(levels)):
        step = 1 << k
        need[k] = sorted(set(need[k + 1]) | {e + step for e in need[k + 1] if e + step < width})
    return [[e for e in need[k + 1] if e + step < width] for k, step in enumerate(1 << k for k in range(levels))]


def reduce_kernel(stages, count, width, terms_ref, out_ref, pair_in, held, *rest):
    depth = len(stages)
    send_bufs, recv_bufs = rest[:depth], rest[depth : 2 * depth]
    last_buf, send_sem, recv_sem = rest[2 * depth], rest[2 * depth + 1], rest[2 * depth + 2]
    me = lax.axis_index("ctx")
    core = me % 2
    chip = me // 2
    chips = count // 2
    handoff = pltpu.make_async_remote_copy(
        src_ref=terms_ref,
        dst_ref=pair_in,
        send_sem=send_sem.at[depth],
        recv_sem=recv_sem.at[depth],
        device_id={"ctx": (me - 1 + count) % count},
        device_id_type=pl.DeviceIdType.MESH,
    )
    back = pltpu.make_async_remote_copy(
        src_ref=held.at[0, 1],
        dst_ref=last_buf,
        send_sem=send_sem.at[depth + 1],
        recv_sem=recv_sem.at[depth + 1],
        device_id={"ctx": (me + 1) % count},
        device_id_type=pl.DeviceIdType.MESH,
    )

    @pl.when(core == 1)
    def _():
        handoff.start()
        handoff.wait_send()

    @pl.when(core == 0)
    def _():
        held[...] = jnp.zeros(held.shape, jnp.float32)
        handoff.wait_recv()
        for d in range(width):
            own_e, own_half = (d + 1) // 2, d % 2
            held[own_e, own_half] = held[own_e, own_half] + terms_ref[d]
            peer_e, peer_half = d // 2, 1 - d % 2
            held[peer_e, peer_half] = held[peer_e, peer_half] + pair_in[d]
        for k, pairs in enumerate(stages):
            step = 1 << k
            copy = pltpu.make_async_remote_copy(
                src_ref=send_bufs[k],
                dst_ref=recv_bufs[k],
                send_sem=send_sem.at[k],
                recv_sem=recv_sem.at[k],
                device_id={"ctx": (me - 2 * step + count) % count},
                device_id_type=pl.DeviceIdType.MESH,
            )

            @pl.when(chip >= step)
            def _():
                for i, e in enumerate(pairs):
                    send_bufs[k][i] = held[e + step].astype(jnp.bfloat16)
                copy.start()

            @pl.when(chip + step < chips)
            def _():
                copy.wait_recv()
                for i, e in enumerate(pairs):
                    held[e] = held[e] + recv_bufs[k][i].astype(jnp.float32)

            @pl.when(chip >= step)
            def _():
                copy.wait_send()

        back.start()
        out_ref[...] = held[0, 0]
        back.wait_send()

    @pl.when(core == 1)
    def _():
        back.wait_recv()
        out_ref[...] = last_buf[...]


def window_reduce(terms, axis):
    width, tokens, cols = terms.shape
    count = lax.axis_size(axis)
    pair_width = width // 2 + 1
    stages = [p for k, p in enumerate(window_stages(pair_width)) if (1 << k) < count // 2]
    vmem = pl.BlockSpec(memory_space=pltpu.VMEM)
    bufs = [pltpu.VMEM((len(p), 2, tokens, cols), jnp.bfloat16) for p in stages]
    return pl.pallas_call(
        functools.partial(reduce_kernel, stages, count, width),
        out_shape=jax.ShapeDtypeStruct((tokens, cols), jnp.float32),
        in_specs=[vmem],
        out_specs=vmem,
        scratch_shapes=[
            pltpu.VMEM((width, tokens, cols), jnp.float32),
            pltpu.VMEM((pair_width, 2, tokens, cols), jnp.float32),
        ]
        + bufs
        + bufs
        + [
            pltpu.VMEM((tokens, cols), jnp.float32),
            pltpu.SemaphoreType.DMA((len(stages) + 2,)),
            pltpu.SemaphoreType.DMA((len(stages) + 2,)),
        ],
        compiler_params=pltpu.CompilerParams(has_side_effects=True),
    )(terms)


def body(
    record_lengths,
    query_heads,
    key_heads,
    value_heads,
    out_grad,
    gate_input,
    key_input,
    value_input,
    hyena_grad,
    short_filter,
    long_filter,
):
    tp = lax.axis_size("tp")
    rows = query_heads.shape[0]

    def exchange(pieces):
        widths = [x.shape[1] // tp for x in pieces]
        joined = jnp.concatenate([x.reshape(rows, tp, w) for x, w in zip(pieces, widths)], axis=2)
        joined = lax.all_to_all(joined, "tp", split_axis=1, concat_axis=0, tiled=True)
        return joined.reshape(rows * tp, sum(widths))

    kv_loc = exchange([key_heads, value_heads])
    kv_all = lax.all_gather(kv_loc, "ctx", axis=0, tiled=True)
    qg_loc = exchange([query_heads, out_grad])
    width = query_heads.shape[1] // tp
    q_loc, g_loc = qg_loc[:, :width], qg_loc[:, width:]
    tokens = q_loc.shape[0]
    ends = jnp.cumsum(record_lengths)
    starts = ends - record_lengths

    def start_of(positions):
        seg = jnp.sum((starts[None, :] <= positions[:, None]).astype(jnp.int32), axis=1) - 1
        return jnp.take(starts, seg)

    own = lax.axis_index("ctx")
    q_start = own * tokens
    q_pos = q_start + jnp.arange(tokens, dtype=jnp.int32)
    q_rec = start_of(q_pos)
    window = (MOST - 1) // tokens + 2
    first = jnp.maximum(q_rec[0] // tokens, own - (window - 1))
    bounds = jnp.stack([first, own]).astype(jnp.int32)
    attn_out, grad_query, terms = attention_local(
        bounds, q_loc, g_loc, kv_all, q_pos[:, None], q_rec[:, None], window
    )
    key_grads = window_reduce(terms, "ctx")
    grad_key = key_grads[:HD].T.astype(jnp.bfloat16)
    grad_value = key_grads[HD:].T.astype(jnp.bfloat16)
    streams = jnp.stack([gate_input, key_input, value_input, hyena_grad], axis=1)
    padded = padded_2(streams, (("ctx", 0),), HALO)
    hyena_val, grad_gate, grad_keyx, grad_valuex = hyena_local(
        padded, short_filter, long_filter, streams.shape[0]
    )
    return (
        attn_out,
        grad_query,
        grad_key,
        grad_value,
        hyena_val,
        grad_gate,
        grad_keyx,
        grad_valuex,
    )


def solution(mesh):
    placed = (
        P(),
        P(("ctx", "tp"), None),
        P(("ctx", "tp"), None),
        P(("ctx", "tp"), None),
        P(("ctx", "tp"), None),
        P("ctx", "tp"),
        P("ctx", "tp"),
        P("ctx", "tp"),
        P("ctx", "tp"),
        P(None, None, "tp"),
        P(None, "tp"),
    )
    return jax.shard_map(
        body,
        mesh=mesh,
        in_specs=placed,
        out_specs=(
            P("ctx", "tp"),
            P("ctx", "tp"),
            P("ctx", "tp"),
            P("ctx", "tp"),
            P("ctx", "tp"),
            P("ctx", "tp"),
            P("ctx", "tp"),
            P("ctx", "tp"),
        ),
        check_vma=False,
    )
```

```python
import functools

import jax
import jax.numpy as jnp
from jax import lax
from jax.experimental import pallas as pl
from jax.experimental.pallas import tpu as pltpu
from jax.sharding import PartitionSpec as P

HD = 128
QH = 64
KVH = 8
GROUP = 16
TAPS = 7
SHORT = 3
HALO = 8
MOST = 3264


NEG = -1e30


def padded_2(cells, sides, width):
    for axis, dim in sides:
        count = lax.axis_size(axis)
        ends = count - 1
        head = lax.slice_in_dim(cells, 0, width, axis=dim)
        tail = lax.slice_in_dim(cells, cells.shape[dim] - width, cells.shape[dim], axis=dim)
        cells = jnp.concatenate(
            [
                lax.ppermute(tail, axis, [(i, (i + 1) % count) for i in range(ends)]),
                cells,
                lax.ppermute(head, axis, [((i + 1) % count, i) for i in range(ends)]),
            ],
            axis=dim,
        )
    return cells


def hyena_local(padded, short_filter, long_filter, tokens):
    wide = padded.astype(jnp.float32)
    rows = wide.shape[0]
    lead = SHORT - 1
    per_channel = jnp.repeat(long_filter, GROUP, axis=1)

    def featurize(values, taps):
        result = taps[0] * values[lead:rows]
        for index in range(1, SHORT):
            result = result + taps[index] * values[lead - index : rows - index]
        return result

    gate_f = featurize(wide[:, 0], short_filter[0])
    key_f = featurize(wide[:, 1], short_filter[1])
    value_f = featurize(wide[:, 2], short_filter[2])
    mixed = key_f * value_f
    offset = HALO - lead
    span = rows - HALO
    conv = per_channel[0] * mixed[offset : offset + span]
    for index in range(1, TAPS):
        conv = conv + per_channel[index] * mixed[offset - index : offset - index + span]
    gate_c = gate_f[offset:]
    grad_c = wide[HALO:, 3]
    hyena_val = (gate_c[:tokens] * conv[:tokens]).astype(jnp.bfloat16)
    dconv = grad_c * gate_c
    dgate_f = grad_c * conv
    dmixed = per_channel[0] * dconv[0 : tokens + lead]
    for index in range(1, TAPS):
        dmixed = dmixed + per_channel[index] * dconv[index : index + tokens + lead]
    key_c = key_f[offset : offset + tokens + lead]
    value_c = value_f[offset : offset + tokens + lead]
    dkey_f = dmixed * value_c
    dvalue_f = dmixed * key_c

    def unfeaturize(grads, taps):
        result = taps[0] * grads[0:tokens]
        for index in range(1, SHORT):
            result = result + taps[index] * grads[index : index + tokens]
        return result.astype(jnp.bfloat16)

    return (
        hyena_val,
        unfeaturize(dgate_f, short_filter[0]),
        unfeaturize(dkey_f, short_filter[1]),
        unfeaturize(dvalue_f, short_filter[2]),
    )


def attention_kernel(
    bounds_ref, q_ref, g_ref, kv_ref, qpos_ref, qstart_ref, qt_ref, gt_ref,
    out_ref, dq_ref, terms_ref,
    qs_ref, gs_ref, m_ref, l_ref, acc_ref, lse_ref, dl_ref, dqa_ref,
):
    tokens = q_ref.shape[0]
    heads = q_ref.shape[1] // HD
    scale = HD ** (-0.5)
    lo = bounds_ref[0]
    hi = bounds_ref[1]
    qpos = qpos_ref[...]
    qstart = qstart_ref[...]
    contract_last = (((1,), (1,)), ((), ()))
    for h in range(heads):
        qs_ref[h * tokens : (h + 1) * tokens, :] = q_ref[:, h * HD : (h + 1) * HD]
        gs_ref[h * tokens : (h + 1) * tokens, :] = g_ref[:, h * HD : (h + 1) * HD]

    def allowed_of(j):
        kpos = j * tokens + lax.broadcasted_iota(jnp.int32, (1, tokens), 1)
        return (kpos <= qpos) & (kpos >= qstart)

    def key_value(j):
        return kv_ref[hi - j, :, 0:HD], kv_ref[hi - j, :, HD : 2 * HD]

    m_ref[...] = jnp.full(m_ref.shape, NEG, jnp.float32)
    l_ref[...] = jnp.zeros(l_ref.shape, jnp.float32)
    acc_ref[...] = jnp.zeros(acc_ref.shape, jnp.float32)

    def forward_block(j, carry):
        key_blk, val_blk = key_value(j)
        allowed = allowed_of(j)
        scores = (
            lax.dot_general(qs_ref[...], key_blk, contract_last, preferred_element_type=jnp.float32)
            * scale
        )
        m_old = m_ref[...]
        m_new = jnp.maximum(m_old, jnp.max(jnp.where(allowed, scores, NEG), axis=1, keepdims=True))
        weights = jnp.where(allowed, jnp.exp(scores - m_new), 0.0)
        factor = jnp.exp(m_old - m_new)
        l_ref[...] = l_ref[...] * factor + jnp.sum(weights, axis=1, keepdims=True)
        acc_ref[...] = acc_ref[...] * factor + jnp.dot(
            weights.astype(jnp.bfloat16), val_blk, preferred_element_type=jnp.float32
        )
        m_ref[...] = m_new
        return carry

    lax.fori_loop(lo, hi + 1, forward_block, 0)

    attn = (acc_ref[...] / l_ref[...]).astype(jnp.bfloat16)
    lse_ref[...] = m_ref[...] + jnp.log(l_ref[...])
    dl_ref[...] = jnp.sum(gs_ref[...].astype(jnp.float32) * attn.astype(jnp.float32), axis=1, keepdims=True)
    for h in range(heads):
        out_ref[:, h * HD : (h + 1) * HD] = attn[h * tokens : (h + 1) * tokens]
    dqa_ref[...] = jnp.zeros(dqa_ref.shape, jnp.float32)
    terms_ref[...] = jnp.zeros(terms_ref.shape, terms_ref.dtype)

    def backward_block(j, carry):
        key_blk, val_blk = key_value(j)
        allowed = allowed_of(j)
        q_all = qs_ref[...]
        g_all = gs_ref[...]
        scores = lax.dot_general(q_all, key_blk, contract_last, preferred_element_type=jnp.float32) * scale
        probs = jnp.where(allowed, jnp.exp(scores - lse_ref[...]), 0.0)
        dv_t = jnp.dot(gt_ref[...], probs.astype(jnp.bfloat16), preferred_element_type=jnp.float32)
        dprobs = lax.dot_general(g_all, val_blk, contract_last, preferred_element_type=jnp.float32)
        dscores = (probs * (dprobs - dl_ref[...])).astype(jnp.bfloat16)
        dqa_ref[...] = dqa_ref[...] + jnp.dot(dscores, key_blk, preferred_element_type=jnp.float32)
        dk_t = jnp.dot(qt_ref[...], dscores, preferred_element_type=jnp.float32)
        terms_ref[hi - j, 0:HD, :] = (dk_t * scale).astype(terms_ref.dtype)
        terms_ref[hi - j, HD : 2 * HD, :] = dv_t.astype(terms_ref.dtype)
        return carry

    lax.fori_loop(lo, hi + 1, backward_block, 0)
    for h in range(heads):
        dq_ref[:, h * HD : (h + 1) * HD] = (
            dqa_ref[h * tokens : (h + 1) * tokens, :] * scale
        ).astype(dq_ref.dtype)


def attention_local(bounds, q_loc, g_loc, kv_all, qpos, qstart, window):
    tokens, width = q_loc.shape
    heads = width // HD
    rows = heads * tokens
    vmem = pl.BlockSpec(memory_space=pltpu.VMEM)
    return pl.pallas_call(
        attention_kernel,
        out_shape=(
            jax.ShapeDtypeStruct((tokens, width), jnp.bfloat16),
            jax.ShapeDtypeStruct((tokens, width), jnp.bfloat16),
            jax.ShapeDtypeStruct((window, 2 * HD, tokens), jnp.float32),
        ),
        in_specs=[pl.BlockSpec(memory_space=pltpu.SMEM)] + [vmem] * 7,
        out_specs=(vmem, vmem, vmem),
        scratch_shapes=[
            pltpu.VMEM((rows, HD), jnp.bfloat16),
            pltpu.VMEM((rows, HD), jnp.bfloat16),
            pltpu.VMEM((rows, 1), jnp.float32),
            pltpu.VMEM((rows, 1), jnp.float32),
            pltpu.VMEM((rows, HD), jnp.float32),
            pltpu.VMEM((rows, 1), jnp.float32),
            pltpu.VMEM((rows, 1), jnp.float32),
            pltpu.VMEM((rows, HD), jnp.float32),
        ],
    )(
        bounds, q_loc, g_loc, kv_all, jnp.tile(qpos, (heads, 1)), jnp.tile(qstart, (heads, 1)),
        heads_major_t(q_loc), heads_major_t(g_loc),
    )


def heads_major_t(x):
    tokens, width = x.shape
    return x.reshape(tokens, width // HD, HD).transpose(2, 1, 0).reshape(HD, width // HD * tokens)


def window_stages(width):
    levels = max(1, (width - 1).bit_length())
    need = [None] * (levels + 1)
    need[levels] = [0]
    for k in reversed(range(levels)):
        step = 1 << k
        need[k] = sorted(set(need[k + 1]) | {e + step for e in need[k + 1] if e + step < width})
    return [[e for e in need[k + 1] if e + step < width] for k, step in enumerate(1 << k for k in range(levels))]


def reduce_kernel(stages, count, terms_ref, out_ref, held, *rest):
    depth = len(stages)
    send_bufs, recv_bufs = rest[:depth], rest[depth : 2 * depth]
    send_sem, recv_sem = rest[2 * depth], rest[2 * depth + 1]
    me = lax.axis_index("ctx")
    held[...] = terms_ref[...]
    for k, pairs in enumerate(stages):
        step = 1 << k
        copy = pltpu.make_async_remote_copy(
            src_ref=send_bufs[k],
            dst_ref=recv_bufs[k],
            send_sem=send_sem.at[k],
            recv_sem=recv_sem.at[k],
            device_id={"ctx": (me - step + count) % count},
            device_id_type=pl.DeviceIdType.MESH,
        )

        @pl.when(me >= step)
        def _():
            for i, e in enumerate(pairs):
                send_bufs[k][i] = held[e + step].astype(jnp.bfloat16)
            copy.start()

        @pl.when(me + step < count)
        def _():
            copy.wait_recv()
            for i, e in enumerate(pairs):
                held[e] = held[e] + recv_bufs[k][i].astype(jnp.float32)

        @pl.when(me >= step)
        def _():
            copy.wait_send()

    out_ref[...] = held[0]


def window_reduce(terms, axis):
    width, tokens, cols = terms.shape
    count = lax.axis_size(axis)
    stages = [pairs for k, pairs in enumerate(window_stages(width)) if (1 << k) < count]
    vmem = pl.BlockSpec(memory_space=pltpu.VMEM)
    bufs = [pltpu.VMEM((len(p), tokens, cols), jnp.bfloat16) for p in stages]
    return pl.pallas_call(
        functools.partial(reduce_kernel, stages, count),
        out_shape=jax.ShapeDtypeStruct((tokens, cols), jnp.float32),
        in_specs=[vmem],
        out_specs=vmem,
        scratch_shapes=[pltpu.VMEM((width, tokens, cols), jnp.float32)]
        + bufs
        + bufs
        + [pltpu.SemaphoreType.DMA((len(stages),)), pltpu.SemaphoreType.DMA((len(stages),))],
        compiler_params=pltpu.CompilerParams(has_side_effects=True),
    )(terms)


def gather_kernel(count, width, own_ref, out_ref, held, send_sem, recv_sem):
    me = lax.axis_index("ctx")
    held[0] = own_ref[...]
    k = 0
    while (1 << k) < min(width, count):
        step = 1 << k
        size = min(step, width - step)
        copy = pltpu.make_async_remote_copy(
            src_ref=held.at[pl.ds(0, size)],
            dst_ref=held.at[pl.ds(step, size)],
            send_sem=send_sem.at[k],
            recv_sem=recv_sem.at[k],
            device_id={"ctx": (me + step) % count},
            device_id_type=pl.DeviceIdType.MESH,
        )

        @pl.when(me + step < count)
        def _():
            copy.start()

        @pl.when(me >= step)
        def _():
            copy.wait_recv()

        @pl.when(me + step < count)
        def _():
            copy.wait_send()

        k += 1
    out_ref[...] = held[...]


def window_gather(own, axis, width):
    count = lax.axis_size(axis)
    stages = 0
    while (1 << stages) < min(width, count):
        stages += 1
    vmem = pl.BlockSpec(memory_space=pltpu.VMEM)
    return pl.pallas_call(
        functools.partial(gather_kernel, count, width),
        out_shape=jax.ShapeDtypeStruct((width,) + own.shape, own.dtype),
        in_specs=[vmem],
        out_specs=vmem,
        scratch_shapes=[
            pltpu.VMEM((width,) + own.shape, own.dtype),
            pltpu.SemaphoreType.DMA((stages,)),
            pltpu.SemaphoreType.DMA((stages,)),
        ],
        compiler_params=pltpu.CompilerParams(has_side_effects=True),
    )(own)


def body(
    record_lengths,
    query_heads,
    key_heads,
    value_heads,
    out_grad,
    gate_input,
    key_input,
    value_input,
    hyena_grad,
    short_filter,
    long_filter,
):
    tp = lax.axis_size("tp")
    rows = query_heads.shape[0]

    def exchange(pieces):
        widths = [x.shape[1] // tp for x in pieces]
        joined = jnp.concatenate([x.reshape(rows, tp, w) for x, w in zip(pieces, widths)], axis=2)
        joined = lax.all_to_all(joined, "tp", split_axis=1, concat_axis=0, tiled=True)
        return joined.reshape(rows * tp, sum(widths))

    kv_loc = exchange([key_heads, value_heads])
    qg_loc = exchange([query_heads, out_grad])
    width = query_heads.shape[1] // tp
    q_loc, g_loc = qg_loc[:, :width], qg_loc[:, width:]
    tokens = q_loc.shape[0]
    ends = jnp.cumsum(record_lengths)
    starts = ends - record_lengths

    def start_of(positions):
        seg = jnp.sum((starts[None, :] <= positions[:, None]).astype(jnp.int32), axis=1) - 1
        return jnp.take(starts, seg)

    own = lax.axis_index("ctx")
    q_start = own * tokens
    q_pos = q_start + jnp.arange(tokens, dtype=jnp.int32)
    q_rec = start_of(q_pos)
    window = (MOST - 1) // tokens + 2
    kv_all = window_gather(kv_loc, "ctx", window)
    first = jnp.maximum(q_rec[0] // tokens, own - (window - 1))
    bounds = jnp.stack([first, own]).astype(jnp.int32)
    attn_out, grad_query, terms = attention_local(
        bounds, q_loc, g_loc, kv_all, q_pos[:, None], q_rec[:, None], window
    )
    key_grads = window_reduce(terms, "ctx")
    grad_key = key_grads[:HD].T.astype(jnp.bfloat16)
    grad_value = key_grads[HD:].T.astype(jnp.bfloat16)
    streams = jnp.stack([gate_input, key_input, value_input, hyena_grad], axis=1)
    padded = padded_2(streams, (("ctx", 0),), HALO)
    hyena_val, grad_gate, grad_keyx, grad_valuex = hyena_local(
        padded, short_filter, long_filter, streams.shape[0]
    )
    return (
        attn_out,
        grad_query,
        grad_key,
        grad_value,
        hyena_val,
        grad_gate,
        grad_keyx,
        grad_valuex,
    )


def solution(mesh):
    placed = (
        P(),
        P(("ctx", "tp"), None),
        P(("ctx", "tp"), None),
        P(("ctx", "tp"), None),
        P(("ctx", "tp"), None),
        P("ctx", "tp"),
        P("ctx", "tp"),
        P("ctx", "tp"),
        P("ctx", "tp"),
        P(None, None, "tp"),
        P(None, "tp"),
    )
    return jax.shard_map(
        body,
        mesh=mesh,
        in_specs=placed,
        out_specs=(
            P("ctx", "tp"),
            P("ctx", "tp"),
            P("ctx", "tp"),
            P("ctx", "tp"),
            P("ctx", "tp"),
            P("ctx", "tp"),
            P("ctx", "tp"),
            P("ctx", "tp"),
        ),
        check_vma=False,
    )
```

```python
import functools

import jax
import jax.numpy as jnp
from jax import lax
from jax.experimental import pallas as pl
from jax.experimental.pallas import tpu as pltpu
from jax.sharding import PartitionSpec as P

HD = 128
QH = 64
KVH = 8
GROUP = 16
TAPS = 7
SHORT = 3
HALO = 8
MOST = 3264


NEG = -1e30


def padded_2(cells, sides, width):
    for axis, dim in sides:
        count = lax.axis_size(axis)
        ends = count - 1
        head = lax.slice_in_dim(cells, 0, width, axis=dim)
        tail = lax.slice_in_dim(cells, cells.shape[dim] - width, cells.shape[dim], axis=dim)
        cells = jnp.concatenate(
            [
                lax.ppermute(tail, axis, [(i, (i + 1) % count) for i in range(ends)]),
                cells,
                lax.ppermute(head, axis, [((i + 1) % count, i) for i in range(ends)]),
            ],
            axis=dim,
        )
    return cells


def hyena_local(padded, short_filter, long_filter, tokens):
    wide = padded.astype(jnp.float32)
    rows = wide.shape[0]
    lead = SHORT - 1
    per_channel = jnp.repeat(long_filter, GROUP, axis=1)

    def featurize(values, taps):
        result = taps[0] * values[lead:rows]
        for index in range(1, SHORT):
            result = result + taps[index] * values[lead - index : rows - index]
        return result

    gate_f = featurize(wide[:, 0], short_filter[0])
    key_f = featurize(wide[:, 1], short_filter[1])
    value_f = featurize(wide[:, 2], short_filter[2])
    mixed = key_f * value_f
    offset = HALO - lead
    span = rows - HALO
    conv = per_channel[0] * mixed[offset : offset + span]
    for index in range(1, TAPS):
        conv = conv + per_channel[index] * mixed[offset - index : offset - index + span]
    gate_c = gate_f[offset:]
    grad_c = wide[HALO:, 3]
    hyena_val = (gate_c[:tokens] * conv[:tokens]).astype(jnp.bfloat16)
    dconv = grad_c * gate_c
    dgate_f = grad_c * conv
    dmixed = per_channel[0] * dconv[0 : tokens + lead]
    for index in range(1, TAPS):
        dmixed = dmixed + per_channel[index] * dconv[index : index + tokens + lead]
    key_c = key_f[offset : offset + tokens + lead]
    value_c = value_f[offset : offset + tokens + lead]
    dkey_f = dmixed * value_c
    dvalue_f = dmixed * key_c

    def unfeaturize(grads, taps):
        result = taps[0] * grads[0:tokens]
        for index in range(1, SHORT):
            result = result + taps[index] * grads[index : index + tokens]
        return result.astype(jnp.bfloat16)

    return (
        hyena_val,
        unfeaturize(dgate_f, short_filter[0]),
        unfeaturize(dkey_f, short_filter[1]),
        unfeaturize(dvalue_f, short_filter[2]),
    )


def attention_kernel(
    bounds_ref, q_ref, g_ref, kv_ref, qpos_ref, qstart_ref,
    out_ref, dq_ref, terms_ref,
    qs_ref, gs_ref, m_ref, l_ref, acc_ref, lse_ref, dl_ref, dqa_ref,
):
    tokens = q_ref.shape[0]
    heads = q_ref.shape[1] // HD
    scale = HD ** (-0.5)
    lo = bounds_ref[0]
    hi = bounds_ref[1]
    qpos = qpos_ref[...]
    qstart = qstart_ref[...]
    contract_last = (((1,), (1,)), ((), ()))
    contract_first = (((0,), (0,)), ((), ()))
    for h in range(heads):
        qs_ref[h * tokens : (h + 1) * tokens, :] = q_ref[:, h * HD : (h + 1) * HD]
        gs_ref[h * tokens : (h + 1) * tokens, :] = g_ref[:, h * HD : (h + 1) * HD]

    def allowed_of(j):
        kpos = j * tokens + lax.broadcasted_iota(jnp.int32, (1, tokens), 1)
        return (kpos <= qpos) & (kpos >= qstart)

    def key_value(j):
        rows = pl.ds(pl.multiple_of(j * tokens, 64), tokens)
        return kv_ref[rows, 0:HD], kv_ref[rows, HD : 2 * HD]

    m_ref[...] = jnp.full(m_ref.shape, NEG, jnp.float32)
    l_ref[...] = jnp.zeros(l_ref.shape, jnp.float32)
    acc_ref[...] = jnp.zeros(acc_ref.shape, jnp.float32)

    def forward_block(j, carry):
        key_blk, val_blk = key_value(j)
        allowed = allowed_of(j)
        scores = (
            lax.dot_general(qs_ref[...], key_blk, contract_last, preferred_element_type=jnp.float32)
            * scale
        )
        m_old = m_ref[...]
        m_new = jnp.maximum(m_old, jnp.max(jnp.where(allowed, scores, NEG), axis=1, keepdims=True))
        weights = jnp.where(allowed, jnp.exp(scores - m_new), 0.0)
        factor = jnp.exp(m_old - m_new)
        l_ref[...] = l_ref[...] * factor + jnp.sum(weights, axis=1, keepdims=True)
        acc_ref[...] = acc_ref[...] * factor + jnp.dot(
            weights.astype(jnp.bfloat16), val_blk, preferred_element_type=jnp.float32
        )
        m_ref[...] = m_new
        return carry

    lax.fori_loop(lo, hi + 1, forward_block, 0)

    attn = (acc_ref[...] / l_ref[...]).astype(jnp.bfloat16)
    lse_ref[...] = m_ref[...] + jnp.log(l_ref[...])
    dl_ref[...] = jnp.sum(gs_ref[...].astype(jnp.float32) * attn.astype(jnp.float32), axis=1, keepdims=True)
    for h in range(heads):
        out_ref[:, h * HD : (h + 1) * HD] = attn[h * tokens : (h + 1) * tokens]
    dqa_ref[...] = jnp.zeros(dqa_ref.shape, jnp.float32)
    terms_ref[...] = jnp.zeros(terms_ref.shape, terms_ref.dtype)

    def backward_block(j, carry):
        key_blk, val_blk = key_value(j)
        allowed = allowed_of(j)
        q_all = qs_ref[...]
        g_all = gs_ref[...]
        scores = lax.dot_general(q_all, key_blk, contract_last, preferred_element_type=jnp.float32) * scale
        probs = jnp.where(allowed, jnp.exp(scores - lse_ref[...]), 0.0)
        dv = lax.dot_general(
            probs.astype(jnp.bfloat16), g_all, contract_first, preferred_element_type=jnp.float32
        )
        dprobs = lax.dot_general(g_all, val_blk, contract_last, preferred_element_type=jnp.float32)
        dscores = (probs * (dprobs - dl_ref[...])).astype(jnp.bfloat16)
        dqa_ref[...] = dqa_ref[...] + jnp.dot(dscores, key_blk, preferred_element_type=jnp.float32)
        dk = lax.dot_general(dscores, q_all, contract_first, preferred_element_type=jnp.float32)
        slot = hi - j
        place = jnp.where(slot % 2 == 1, (slot - 1) // 2, terms_ref.shape[0] // 2 + slot // 2)
        terms_ref[place, :, 0:HD] = (dk * scale).astype(terms_ref.dtype)
        terms_ref[place, :, HD : 2 * HD] = dv.astype(terms_ref.dtype)
        return carry

    lax.fori_loop(lo, hi + 1, backward_block, 0)
    for h in range(heads):
        dq_ref[:, h * HD : (h + 1) * HD] = (
            dqa_ref[h * tokens : (h + 1) * tokens, :] * scale
        ).astype(dq_ref.dtype)


def attention_local(bounds, q_loc, g_loc, kv_all, qpos, qstart, window):
    tokens, width = q_loc.shape
    heads = width // HD
    rows = heads * tokens
    vmem = pl.BlockSpec(memory_space=pltpu.VMEM)
    return pl.pallas_call(
        attention_kernel,
        out_shape=(
            jax.ShapeDtypeStruct((tokens, width), jnp.bfloat16),
            jax.ShapeDtypeStruct((tokens, width), jnp.bfloat16),
            jax.ShapeDtypeStruct((window, tokens, 2 * HD), jnp.bfloat16),
        ),
        in_specs=[pl.BlockSpec(memory_space=pltpu.SMEM)] + [vmem] * 5,
        out_specs=(vmem, vmem, vmem),
        scratch_shapes=[
            pltpu.VMEM((rows, HD), jnp.bfloat16),
            pltpu.VMEM((rows, HD), jnp.bfloat16),
            pltpu.VMEM((rows, 1), jnp.float32),
            pltpu.VMEM((rows, 1), jnp.float32),
            pltpu.VMEM((rows, HD), jnp.float32),
            pltpu.VMEM((rows, 1), jnp.float32),
            pltpu.VMEM((rows, 1), jnp.float32),
            pltpu.VMEM((rows, HD), jnp.float32),
        ],
    )(bounds, q_loc, g_loc, kv_all, jnp.tile(qpos, (heads, 1)), jnp.tile(qstart, (heads, 1)))


def window_stages(width):
    levels = max(1, (width - 1).bit_length())
    need = [None] * (levels + 1)
    need[levels] = [0]
    for k in reversed(range(levels)):
        step = 1 << k
        need[k] = sorted(set(need[k + 1]) | {e + step for e in need[k + 1] if e + step < width})
    return [[e for e in need[k + 1] if e + step < width] for k, step in enumerate(1 << k for k in range(levels))]


def reduce_kernel(stages, count, terms_ref, out_ref, held, *rest):
    depth = len(stages)
    send_bufs, recv_bufs = rest[:depth], rest[depth : 2 * depth]
    send_sem, recv_sem = rest[2 * depth], rest[2 * depth + 1]
    me = lax.axis_index("ctx")
    width = terms_ref.shape[0]
    odd = width // 2
    for k, pairs in enumerate(stages):
        step = 1 << k
        copy = pltpu.make_async_remote_copy(
            src_ref=terms_ref.at[pl.ds(0, odd)] if k == 0 else send_bufs[k],
            dst_ref=recv_bufs[k],
            send_sem=send_sem.at[k],
            recv_sem=recv_sem.at[k],
            device_id={"ctx": (me - step + count) % count},
            device_id_type=pl.DeviceIdType.MESH,
        )

        @pl.when(me >= step)
        def _():
            if k > 0:
                for i, e in enumerate(pairs):
                    send_bufs[k][i] = held[e + step].astype(jnp.bfloat16)
            copy.start()

        if k == 0:
            for d in range(width):
                place = (d - 1) // 2 if d % 2 else odd + d // 2
                held[d] = terms_ref[place].astype(jnp.float32)

        @pl.when(me + step < count)
        def _():
            copy.wait_recv()
            for i, e in enumerate(pairs):
                held[e] = held[e] + recv_bufs[k][i].astype(jnp.float32)

        @pl.when(me >= step)
        def _():
            copy.wait_send()

    out_ref[...] = held[0]


def window_reduce(terms, axis):
    width, tokens, cols = terms.shape
    count = lax.axis_size(axis)
    stages = [pairs for k, pairs in enumerate(window_stages(width)) if (1 << k) < count]
    vmem = pl.BlockSpec(memory_space=pltpu.VMEM)
    assert stages[0] == list(range(0, width - 1, 2))
    bufs = [pltpu.VMEM((len(p), tokens, cols), jnp.bfloat16) for p in stages]
    return pl.pallas_call(
        functools.partial(reduce_kernel, stages, count),
        out_shape=jax.ShapeDtypeStruct((tokens, cols), jnp.float32),
        in_specs=[vmem],
        out_specs=vmem,
        scratch_shapes=[pltpu.VMEM((width, tokens, cols), jnp.float32)]
        + bufs
        + bufs
        + [pltpu.SemaphoreType.DMA((len(stages),)), pltpu.SemaphoreType.DMA((len(stages),))],
        compiler_params=pltpu.CompilerParams(has_side_effects=True),
    )(terms)


def body(
    record_lengths,
    query_heads,
    key_heads,
    value_heads,
    out_grad,
    gate_input,
    key_input,
    value_input,
    hyena_grad,
    short_filter,
    long_filter,
):
    tp = lax.axis_size("tp")
    rows = query_heads.shape[0]

    def exchange(pieces):
        widths = [x.shape[1] // tp for x in pieces]
        joined = jnp.concatenate([x.reshape(rows, tp, w) for x, w in zip(pieces, widths)], axis=2)
        joined = lax.all_to_all(joined, "tp", split_axis=1, concat_axis=0, tiled=True)
        return joined.reshape(rows * tp, sum(widths))

    kv_loc = exchange([key_heads, value_heads])
    kv_all = lax.all_gather(kv_loc, "ctx", axis=0, tiled=True)
    qg_loc = exchange([query_heads, out_grad])
    width = query_heads.shape[1] // tp
    q_loc, g_loc = qg_loc[:, :width], qg_loc[:, width:]
    tokens = q_loc.shape[0]
    ends = jnp.cumsum(record_lengths)
    starts = ends - record_lengths

    def start_of(positions):
        seg = jnp.sum((starts[None, :] <= positions[:, None]).astype(jnp.int32), axis=1) - 1
        return jnp.take(starts, seg)

    own = lax.axis_index("ctx")
    q_start = own * tokens
    q_pos = q_start + jnp.arange(tokens, dtype=jnp.int32)
    q_rec = start_of(q_pos)
    window = (MOST - 1) // tokens + 2
    first = jnp.maximum(q_rec[0] // tokens, own - (window - 1))
    bounds = jnp.stack([first, own]).astype(jnp.int32)
    attn_out, grad_query, terms = attention_local(
        bounds, q_loc, g_loc, kv_all, q_pos[:, None], q_rec[:, None], window
    )
    key_grads = window_reduce(terms, "ctx")
    grad_key = key_grads[:, :HD].astype(jnp.bfloat16)
    grad_value = key_grads[:, HD:].astype(jnp.bfloat16)
    streams = jnp.stack([gate_input, key_input, value_input, hyena_grad], axis=1)
    padded = padded_2(streams, (("ctx", 0),), HALO)
    hyena_val, grad_gate, grad_keyx, grad_valuex = hyena_local(
        padded, short_filter, long_filter, streams.shape[0]
    )
    return (
        attn_out,
        grad_query,
        grad_key,
        grad_value,
        hyena_val,
        grad_gate,
        grad_keyx,
        grad_valuex,
    )


def solution(mesh):
    placed = (
        P(),
        P(("ctx", "tp"), None),
        P(("ctx", "tp"), None),
        P(("ctx", "tp"), None),
        P(("ctx", "tp"), None),
        P("ctx", "tp"),
        P("ctx", "tp"),
        P("ctx", "tp"),
        P("ctx", "tp"),
        P(None, None, "tp"),
        P(None, "tp"),
    )
    return jax.shard_map(
        body,
        mesh=mesh,
        in_specs=placed,
        out_specs=(
            P("ctx", "tp"),
            P("ctx", "tp"),
            P("ctx", "tp"),
            P("ctx", "tp"),
            P("ctx", "tp"),
            P("ctx", "tp"),
            P("ctx", "tp"),
            P("ctx", "tp"),
        ),
        check_vma=False,
    )
```

```python
import functools

import jax
import jax.numpy as jnp
from jax import lax
from jax.experimental import pallas as pl
from jax.experimental.pallas import tpu as pltpu
from jax.sharding import PartitionSpec as P

HD = 128
QH = 64
KVH = 8
GROUP = 16
TAPS = 7
SHORT = 3
HALO = 8
MOST = 3264


NEG = -1e30


def padded_2(cells, sides, width):
    for axis, dim in sides:
        count = lax.axis_size(axis)
        ends = count - 1
        head = lax.slice_in_dim(cells, 0, width, axis=dim)
        tail = lax.slice_in_dim(cells, cells.shape[dim] - width, cells.shape[dim], axis=dim)
        cells = jnp.concatenate(
            [
                lax.ppermute(tail, axis, [(i, (i + 1) % count) for i in range(ends)]),
                cells,
                lax.ppermute(head, axis, [((i + 1) % count, i) for i in range(ends)]),
            ],
            axis=dim,
        )
    return cells


def hyena_local(padded, short_filter, long_filter, tokens):
    wide = padded.astype(jnp.float32)
    rows = wide.shape[0]
    lead = SHORT - 1
    per_channel = jnp.repeat(long_filter, GROUP, axis=1)

    def featurize(values, taps):
        result = taps[0] * values[lead:rows]
        for index in range(1, SHORT):
            result = result + taps[index] * values[lead - index : rows - index]
        return result

    gate_f = featurize(wide[:, 0], short_filter[0])
    key_f = featurize(wide[:, 1], short_filter[1])
    value_f = featurize(wide[:, 2], short_filter[2])
    mixed = key_f * value_f
    offset = HALO - lead
    span = rows - HALO
    conv = per_channel[0] * mixed[offset : offset + span]
    for index in range(1, TAPS):
        conv = conv + per_channel[index] * mixed[offset - index : offset - index + span]
    gate_c = gate_f[offset:]
    grad_c = wide[HALO:, 3]
    hyena_val = (gate_c[:tokens] * conv[:tokens]).astype(jnp.bfloat16)
    dconv = grad_c * gate_c
    dgate_f = grad_c * conv
    dmixed = per_channel[0] * dconv[0 : tokens + lead]
    for index in range(1, TAPS):
        dmixed = dmixed + per_channel[index] * dconv[index : index + tokens + lead]
    key_c = key_f[offset : offset + tokens + lead]
    value_c = value_f[offset : offset + tokens + lead]
    dkey_f = dmixed * value_c
    dvalue_f = dmixed * key_c

    def unfeaturize(grads, taps):
        result = taps[0] * grads[0:tokens]
        for index in range(1, SHORT):
            result = result + taps[index] * grads[index : index + tokens]
        return result.astype(jnp.bfloat16)

    return (
        hyena_val,
        unfeaturize(dgate_f, short_filter[0]),
        unfeaturize(dkey_f, short_filter[1]),
        unfeaturize(dvalue_f, short_filter[2]),
    )


def attention_kernel(
    bounds_ref, q_ref, g_ref, kv_ref, qpos_ref, qstart_ref, qt_ref, gt_ref,
    out_ref, dq_ref, terms_ref,
    qs_ref, gs_ref, m_ref, l_ref, acc_ref, lse_ref, dl_ref, dqa_ref,
):
    tokens = q_ref.shape[0]
    heads = q_ref.shape[1] // HD
    scale = HD ** (-0.5)
    lo = bounds_ref[0]
    hi = bounds_ref[1]
    qpos = qpos_ref[...]
    qstart = qstart_ref[...]
    contract_last = (((1,), (1,)), ((), ()))
    for h in range(heads):
        qs_ref[h * tokens : (h + 1) * tokens, :] = q_ref[:, h * HD : (h + 1) * HD]
        gs_ref[h * tokens : (h + 1) * tokens, :] = g_ref[:, h * HD : (h + 1) * HD]

    def allowed_of(j):
        kpos = j * tokens + lax.broadcasted_iota(jnp.int32, (1, tokens), 1)
        return (kpos <= qpos) & (kpos >= qstart)

    def key_value(j):
        rows = pl.ds(pl.multiple_of(j * tokens, 64), tokens)
        return kv_ref[rows, 0:HD], kv_ref[rows, HD : 2 * HD]

    m_ref[...] = jnp.full(m_ref.shape, NEG, jnp.float32)
    l_ref[...] = jnp.zeros(l_ref.shape, jnp.float32)
    acc_ref[...] = jnp.zeros(acc_ref.shape, jnp.float32)

    def forward_block(j, carry):
        key_blk, val_blk = key_value(j)
        allowed = allowed_of(j)
        scores = (
            lax.dot_general(qs_ref[...], key_blk, contract_last, preferred_element_type=jnp.float32)
            * scale
        )
        m_old = m_ref[...]
        m_new = jnp.maximum(m_old, jnp.max(jnp.where(allowed, scores, NEG), axis=1, keepdims=True))
        weights = jnp.where(allowed, jnp.exp(scores - m_new), 0.0)
        factor = jnp.exp(m_old - m_new)
        l_ref[...] = l_ref[...] * factor + jnp.sum(weights, axis=1, keepdims=True)
        acc_ref[...] = acc_ref[...] * factor + jnp.dot(
            weights.astype(jnp.bfloat16), val_blk, preferred_element_type=jnp.float32
        )
        m_ref[...] = m_new
        return carry

    lax.fori_loop(lo, hi + 1, forward_block, 0)

    attn = (acc_ref[...] / l_ref[...]).astype(jnp.bfloat16)
    lse_ref[...] = m_ref[...] + jnp.log(l_ref[...])
    dl_ref[...] = jnp.sum(gs_ref[...].astype(jnp.float32) * attn.astype(jnp.float32), axis=1, keepdims=True)
    for h in range(heads):
        out_ref[:, h * HD : (h + 1) * HD] = attn[h * tokens : (h + 1) * tokens]
    dqa_ref[...] = jnp.zeros(dqa_ref.shape, jnp.float32)
    terms_ref[...] = jnp.zeros(terms_ref.shape, terms_ref.dtype)

    def backward_block(j, carry):
        key_blk, val_blk = key_value(j)
        allowed = allowed_of(j)
        q_all = qs_ref[...]
        g_all = gs_ref[...]
        scores = lax.dot_general(q_all, key_blk, contract_last, preferred_element_type=jnp.float32) * scale
        probs = jnp.where(allowed, jnp.exp(scores - lse_ref[...]), 0.0)
        dv_t = jnp.dot(gt_ref[...], probs.astype(jnp.bfloat16), preferred_element_type=jnp.float32)
        dprobs = lax.dot_general(g_all, val_blk, contract_last, preferred_element_type=jnp.float32)
        dscores = (probs * (dprobs - dl_ref[...])).astype(jnp.bfloat16)
        dqa_ref[...] = dqa_ref[...] + jnp.dot(dscores, key_blk, preferred_element_type=jnp.float32)
        dk_t = jnp.dot(qt_ref[...], dscores, preferred_element_type=jnp.float32)
        slot = hi - j
        place = jnp.where(slot % 2 == 1, (slot - 1) // 2, terms_ref.shape[0] // 2 + slot // 2)
        terms_ref[place, 0:HD, :] = (dk_t * scale).astype(terms_ref.dtype)
        terms_ref[place, HD : 2 * HD, :] = dv_t.astype(terms_ref.dtype)
        return carry

    lax.fori_loop(lo, hi + 1, backward_block, 0)
    for h in range(heads):
        dq_ref[:, h * HD : (h + 1) * HD] = (
            dqa_ref[h * tokens : (h + 1) * tokens, :] * scale
        ).astype(dq_ref.dtype)


def attention_local(bounds, q_loc, g_loc, kv_all, qpos, qstart, window):
    tokens, width = q_loc.shape
    heads = width // HD
    rows = heads * tokens
    vmem = pl.BlockSpec(memory_space=pltpu.VMEM)
    return pl.pallas_call(
        attention_kernel,
        out_shape=(
            jax.ShapeDtypeStruct((tokens, width), jnp.bfloat16),
            jax.ShapeDtypeStruct((tokens, width), jnp.bfloat16),
            jax.ShapeDtypeStruct((window, 2 * HD, tokens), jnp.bfloat16),
        ),
        in_specs=[pl.BlockSpec(memory_space=pltpu.SMEM)] + [vmem] * 7,
        out_specs=(vmem, vmem, vmem),
        scratch_shapes=[
            pltpu.VMEM((rows, HD), jnp.bfloat16),
            pltpu.VMEM((rows, HD), jnp.bfloat16),
            pltpu.VMEM((rows, 1), jnp.float32),
            pltpu.VMEM((rows, 1), jnp.float32),
            pltpu.VMEM((rows, HD), jnp.float32),
            pltpu.VMEM((rows, 1), jnp.float32),
            pltpu.VMEM((rows, 1), jnp.float32),
            pltpu.VMEM((rows, HD), jnp.float32),
        ],
    )(
        bounds, q_loc, g_loc, kv_all, jnp.tile(qpos, (heads, 1)), jnp.tile(qstart, (heads, 1)),
        heads_major_t(q_loc), heads_major_t(g_loc),
    )


def heads_major_t(x):
    tokens, width = x.shape
    return x.reshape(tokens, width // HD, HD).transpose(2, 1, 0).reshape(HD, width // HD * tokens)


def window_stages(width):
    levels = max(1, (width - 1).bit_length())
    need = [None] * (levels + 1)
    need[levels] = [0]
    for k in reversed(range(levels)):
        step = 1 << k
        need[k] = sorted(set(need[k + 1]) | {e + step for e in need[k + 1] if e + step < width})
    return [[e for e in need[k + 1] if e + step < width] for k, step in enumerate(1 << k for k in range(levels))]


def reduce_kernel(stages, count, terms_ref, out_ref, held, *rest):
    depth = len(stages)
    send_bufs, recv_bufs = rest[:depth], rest[depth : 2 * depth]
    send_sem, recv_sem = rest[2 * depth], rest[2 * depth + 1]
    me = lax.axis_index("ctx")
    width = terms_ref.shape[0]
    odd = width // 2
    for k, pairs in enumerate(stages):
        step = 1 << k
        copy = pltpu.make_async_remote_copy(
            src_ref=terms_ref.at[pl.ds(0, odd)] if k == 0 else send_bufs[k],
            dst_ref=recv_bufs[k],
            send_sem=send_sem.at[k],
            recv_sem=recv_sem.at[k],
            device_id={"ctx": (me - step + count) % count},
            device_id_type=pl.DeviceIdType.MESH,
        )

        @pl.when(me >= step)
        def _():
            if k > 0:
                for i, e in enumerate(pairs):
                    send_bufs[k][i] = held[e + step].astype(jnp.bfloat16)
            copy.start()

        if k == 0:
            for d in range(width):
                place = (d - 1) // 2 if d % 2 else odd + d // 2
                held[d] = terms_ref[place].astype(jnp.float32)

        @pl.when(me + step < count)
        def _():
            copy.wait_recv()
            for i, e in enumerate(pairs):
                held[e] = held[e] + recv_bufs[k][i].astype(jnp.float32)

        @pl.when(me >= step)
        def _():
            copy.wait_send()

    out_ref[...] = held[0]


def window_reduce(terms, axis):
    width, tokens, cols = terms.shape
    count = lax.axis_size(axis)
    stages = [pairs for k, pairs in enumerate(window_stages(width)) if (1 << k) < count]
    vmem = pl.BlockSpec(memory_space=pltpu.VMEM)
    assert stages[0] == list(range(0, width - 1, 2))
    bufs = [pltpu.VMEM((len(p), tokens, cols), jnp.bfloat16) for p in stages]
    return pl.pallas_call(
        functools.partial(reduce_kernel, stages, count),
        out_shape=jax.ShapeDtypeStruct((tokens, cols), jnp.float32),
        in_specs=[vmem],
        out_specs=vmem,
        scratch_shapes=[pltpu.VMEM((width, tokens, cols), jnp.float32)]
        + bufs
        + bufs
        + [pltpu.SemaphoreType.DMA((len(stages),)), pltpu.SemaphoreType.DMA((len(stages),))],
        compiler_params=pltpu.CompilerParams(has_side_effects=True),
    )(terms)


def body(
    record_lengths,
    query_heads,
    key_heads,
    value_heads,
    out_grad,
    gate_input,
    key_input,
    value_input,
    hyena_grad,
    short_filter,
    long_filter,
):
    tp = lax.axis_size("tp")
    rows = query_heads.shape[0]

    def exchange(pieces):
        widths = [x.shape[1] // tp for x in pieces]
        joined = jnp.concatenate([x.reshape(rows, tp, w) for x, w in zip(pieces, widths)], axis=2)
        joined = lax.all_to_all(joined, "tp", split_axis=1, concat_axis=0, tiled=True)
        return joined.reshape(rows * tp, sum(widths))

    kv_loc = exchange([key_heads, value_heads])
    kv_all = lax.all_gather(kv_loc, "ctx", axis=0, tiled=True)
    qg_loc = exchange([query_heads, out_grad])
    width = query_heads.shape[1] // tp
    q_loc, g_loc = qg_loc[:, :width], qg_loc[:, width:]
    tokens = q_loc.shape[0]
    ends = jnp.cumsum(record_lengths)
    starts = ends - record_lengths

    def start_of(positions):
        seg = jnp.sum((starts[None, :] <= positions[:, None]).astype(jnp.int32), axis=1) - 1
        return jnp.take(starts, seg)

    own = lax.axis_index("ctx")
    q_start = own * tokens
    q_pos = q_start + jnp.arange(tokens, dtype=jnp.int32)
    q_rec = start_of(q_pos)
    window = (MOST - 1) // tokens + 2
    first = jnp.maximum(q_rec[0] // tokens, own - (window - 1))
    bounds = jnp.stack([first, own]).astype(jnp.int32)
    attn_out, grad_query, terms = attention_local(
        bounds, q_loc, g_loc, kv_all, q_pos[:, None], q_rec[:, None], window
    )
    key_grads = window_reduce(terms, "ctx")
    grad_key = key_grads[:HD].T.astype(jnp.bfloat16)
    grad_value = key_grads[HD:].T.astype(jnp.bfloat16)
    streams = jnp.stack([gate_input, key_input, value_input, hyena_grad], axis=1)
    padded = padded_2(streams, (("ctx", 0),), HALO)
    hyena_val, grad_gate, grad_keyx, grad_valuex = hyena_local(
        padded, short_filter, long_filter, streams.shape[0]
    )
    return (
        attn_out,
        grad_query,
        grad_key,
        grad_value,
        hyena_val,
        grad_gate,
        grad_keyx,
        grad_valuex,
    )


def solution(mesh):
    placed = (
        P(),
        P(("ctx", "tp"), None),
        P(("ctx", "tp"), None),
        P(("ctx", "tp"), None),
        P(("ctx", "tp"), None),
        P("ctx", "tp"),
        P("ctx", "tp"),
        P("ctx", "tp"),
        P("ctx", "tp"),
        P(None, None, "tp"),
        P(None, "tp"),
    )
    return jax.shard_map(
        body,
        mesh=mesh,
        in_specs=placed,
        out_specs=(
            P("ctx", "tp"),
            P("ctx", "tp"),
            P("ctx", "tp"),
            P("ctx", "tp"),
            P("ctx", "tp"),
            P("ctx", "tp"),
            P("ctx", "tp"),
            P("ctx", "tp"),
        ),
        check_vma=False,
    )
```
